32 devices in a mesh: expert: 8 (over z, y), tensor: 4 (over x, core).
Axes of the slice: x: 2, y: 2, z: 4, core: 2. Of those that a mesh axis runs over, the one named last changes fastest.
Arguments:
- tokens: bfloat16 [1024, 7168], P('expert', 'tensor'), may hold values from -6 to 6
- upstream: bfloat16 [1024, 7168], P('expert', 'tensor'), may hold values from -6 to 6
- gates: float32 [1024, 2], P('expert'), may hold values from 0.25 to 1
- expert_ids: int32 [1024, 2], P('expert'), may hold values from 0 to 7, all different within a row; in each aligned block of 128 rows (0 to 127, 128 to 255, ...) at most 48 rows name the same one
- w_gate: bfloat16 [8, 7168, 1024], P('expert', None, 'tensor'), may hold values from -0.0625 to 0.0625
- w_up: bfloat16 [8, 7168, 1024], P('expert', None, 'tensor'), may hold values from -0.0625 to 0.0625
- w_down: bfloat16 [8, 1024, 7168], P('expert', 'tensor'), may hold values from -0.1875 to 0.1875
Outputs:
- mixed: bfloat16 [1024, 7168], P('expert', 'tensor')
- grad_tokens: bfloat16 [1024, 7168], P('expert', 'tensor')
- gate_grads: float32 [1024, 2], P('expert')
The draws below stay inside these ranges and needn't reach their ends.
Inputs may be any that keep to these rules, and one draw needn't show every extreme that they name: `expert_ids`: each token names two different experts; among the tokens held at one index along the `expert` axis no expert is named more than 48 times, and in every draw some expert is named exactly 48 times there.
All inputs are finite; a program needn't handle non-finite values.
Results may differ from the reference program's by a relative error of at most 0.015.
Values may be sent and summed in bfloat16 or wider, within the bound.
No kernel may reach another device: no remote copies, remote signals or barrier semaphores. Data moves between devices by JAX's collectives and lax.ppermute only.
A program may use at most 128 MiB of HBM per device.

```python
import math
import jax
import jax.numpy as jnp
import numpy as np
from jax import lax

D = 7168
FF = 1024
TOK_DEV = 128
EXPERTS = 8
TOKENS = 1024
CAP = 48
N_EXPERT = 8
N_TENSOR = 4


def levels(stream_key, dims, cuts, least, top_value):
    def one(axis_at, parts):
        steps = jax.random.uniform(jax.random.fold_in(jax.random.fold_in(stream_key, 6), axis_at), (parts,), jnp.float32, least / len(cuts), top_value / len(cuts))
        return jnp.repeat(jnp.exp(steps), dims[axis_at] // parts).reshape((-1,) + (1,) * (len(dims) - axis_at - 1))

    factor_of = one(*cuts[0])
    for cut in cuts[1:]:
        factor_of = factor_of * one(*cut)
    return factor_of


def assign_block(key, own, number, rows, number_of, top, limit, slope):
    ranking = jax.random.permutation(key, number_of)
    heavy_load, ordinary = shares(number_of, rows * top, limit, slope, True), shares(number_of, rows * top, limit, slope, False)
    places = jnp.arange(number_of)

    def named(tallies, rotation):
        used = int((tallies > 0).sum())
        fixed = max(1, used // 4)
        shifted = fixed + (places - fixed + rotation * (used - fixed)) % max(1, number_of - fixed)
        return jnp.zeros((number_of,), jnp.int32).at[ranking[jnp.where(places < fixed, places, shifted)]].set(jnp.asarray(tallies, jnp.int32))

    tallies = jnp.where(number % 4 == 0, named(heavy_load, number // 4), named(ordinary, number - number // 4 - 1))
    mixed = jax.random.permutation(jax.random.fold_in(own, 3), number_of)
    donor, receiver = mixed[0:number_of // 2 * 2:2], mixed[1:number_of // 2 * 2:2]
    margin = jnp.minimum(tallies[donor] - 1, limit - tallies[receiver]) // 2
    margin = jnp.where((donor == ranking[0]) | (receiver == ranking[0]) | (tallies[receiver] == 0), 0, jnp.maximum(margin, 0))
    shifted = jax.random.randint(jax.random.fold_in(own, 4), (number_of // 2,), 0, 1 << 20) % (margin + 1)
    tallies = tallies.at[donor].add(-shifted).at[receiver].add(shifted)
    labels = jnp.searchsorted(jnp.cumsum(tallies), jnp.arange(rows * top), side="right").astype(jnp.int32)
    table = labels.reshape(top, rows).T
    table = table[jax.random.permutation(jax.random.fold_in(own, 1), rows)]
    rotation = jax.random.randint(jax.random.fold_in(own, 2), (rows, 1), 0, top)
    return jnp.take_along_axis(table, (jnp.arange(top)[None, :] + rotation) % top, axis=1)


def shares(count, total, most, slope, full):
    loads = [(1 << 20) // math.isqrt(grade ** slope) + 1 for grade in range(1, count + 1)]
    largest = most if full else min(most, max(-(-total // count), total * loads[0] // sum(loads)))
    least = 1 if total - largest >= count - 1 else 0
    holding, surplus = [largest] + [least] * (count - 1), total - largest - least * (count - 1)
    while surplus > 0:
        candidates = [i for i in range(1, count) if holding[i] < largest] or [i for i in range(1, count) if holding[i] < most]
        mass, left = sum([loads[i] for i in candidates]), surplus
        for i in candidates:
            addition = min(most - holding[i], max(1, left * loads[i] // mass), surplus)
            holding[i] = holding[i] + addition
            surplus = surplus - addition
    return np.array(holding)


def scatter_about(own_key, extent, width, limit, cuts=(), held_as=jnp.bfloat16):
    drawn = width * jax.random.normal(own_key, extent, jnp.float32)
    if cuts:
        drawn = drawn * levels(own_key, extent, cuts, -0.22, 0.18)
    return jnp.clip(drawn, -limit, limit).astype(held_as)


def setup_inputs(seed: int = 0) -> dict:
    arg_keys = jax.random.split(jax.random.key(seed), 8)
    tokens = scatter_about(arg_keys[0], (TOKENS, D), 1.0, 6.0, ((0, 8), (1, 4)))
    upstream = scatter_about(arg_keys[1], (TOKENS, D), 1.0, 6.0, ((0, 8), (1, 4)))
    gates = jnp.clip(jnp.exp(math.log(1.0) - 1.3862944 * jax.random.uniform(arg_keys[2], (TOKENS, 2), jnp.float32) ** levels(arg_keys[2], (TOKENS, 2), ((0, 8),), -0.2, 0.2)), 0.25, 1.0)
    expert_ids_keys = jax.random.split(jax.random.fold_in(arg_keys[3], 1), TOKENS // TOK_DEV)
    expert_ids_turns = jax.random.permutation(jax.random.fold_in(arg_keys[3], 3), TOKENS // TOK_DEV)
    expert_ids = jax.vmap(lambda own, number: assign_block(jax.random.fold_in(arg_keys[3], 2), own, number, TOK_DEV, EXPERTS, 2, CAP, 2))(expert_ids_keys, expert_ids_turns).reshape((TOKENS, 2))
    w_gate = scatter_about(arg_keys[4], (EXPERTS, D, FF), D ** -0.5, 0.0625, ((0, 8), (2, 4)))
    w_up = scatter_about(arg_keys[5], (EXPERTS, D, FF), D ** -0.5, 0.0625, ((0, 8), (2, 4)))
    w_down = scatter_about(arg_keys[6], (EXPERTS, FF, D), FF ** -0.5, 0.1875, ((0, 8), (1, 4)))
    return dict(tokens=tokens, upstream=upstream, gates=gates, expert_ids=expert_ids, w_gate=w_gate, w_up=w_up, w_down=w_down)


def rounded(value):
    return lax.optimization_barrier(value.astype(jnp.bfloat16)).astype(jnp.float32)


def matmul(left, right):
    return jnp.dot(left.astype(jnp.float32), right.astype(jnp.float32), precision=lax.Precision.HIGHEST)


def reference(tokens, upstream, gates, expert_ids, w_gate, w_up, w_down):
    source_count = N_EXPERT
    entry_count = 2 * TOK_DEV
    slot_count = EXPERTS * CAP
    group_width = FF // N_TENSOR
    ids_block = expert_ids.reshape(source_count, entry_count)
    onehot = (ids_block[:, :, None] == jnp.arange(EXPERTS, dtype=jnp.int32)[None, None, :]).astype(jnp.int32)
    before = jnp.cumsum(onehot, axis=1) - onehot
    position = jnp.sum(before * onehot, axis=2)
    slot_of_entry = ids_block * CAP + position
    match = slot_of_entry[:, None, :] == jnp.arange(slot_count, dtype=jnp.int32)[None, :, None]
    entry_index = jnp.arange(entry_count, dtype=jnp.int32)
    entry_of_slot = jnp.sum(jnp.where(match, entry_index[None, None, :], 0), axis=2).astype(jnp.int32)
    slot_used = jnp.any(match, axis=2)
    global_entry = jnp.arange(source_count, dtype=jnp.int32)[:, None] * entry_count + entry_of_slot
    global_entry = global_entry.reshape(source_count, EXPERTS, CAP).transpose(1, 0, 2).reshape(EXPERTS, source_count * CAP)
    used_rows = slot_used.reshape(source_count, EXPERTS, CAP).transpose(1, 0, 2).reshape(EXPERTS, source_count * CAP)
    gate_flat = gates.reshape(-1)
    dummy = TOKENS * 2

    def expert_step(carry, inputs):
        out_all, grad_all = carry
        entry_ids, used, weight_gate, weight_up, weight_down = inputs
        token_ids = entry_ids // 2
        row_x = jnp.where(used[:, None], tokens[token_ids], jnp.zeros((), jnp.bfloat16))
        scaled = (upstream[token_ids].astype(jnp.float32) * gate_flat[entry_ids][:, None]).astype(jnp.bfloat16)
        row_dy = jnp.where(used[:, None], scaled, jnp.zeros((), jnp.bfloat16))
        gate_pre = matmul(row_x, weight_gate)
        up_pre = matmul(row_x, weight_up)
        sigma = jax.nn.sigmoid(gate_pre)
        active = gate_pre * sigma
        hidden = (active * up_pre).astype(jnp.bfloat16)
        grad_hidden = matmul(row_dy, weight_down.T)
        grad_up = (grad_hidden * active).astype(jnp.bfloat16)
        grad_gate = (grad_hidden * up_pre * sigma * (1.0 + gate_pre * (1.0 - sigma))).astype(jnp.bfloat16)
        out_sum = jnp.zeros((row_x.shape[0], D), jnp.float32)
        grad_sum = jnp.zeros((row_x.shape[0], D), jnp.float32)
        for group in range(N_TENSOR):
            lower = group * group_width
            upper = lower + group_width
            out_sum = out_sum + rounded(matmul(hidden[:, lower:upper], weight_down[lower:upper]))
            part = matmul(grad_gate[:, lower:upper], weight_gate[:, lower:upper].T)
            part = part + matmul(grad_up[:, lower:upper], weight_up[:, lower:upper].T)
            grad_sum = grad_sum + rounded(part)
        target = jnp.where(used, entry_ids, dummy)
        out_all = out_all.at[target].set(out_sum.astype(jnp.bfloat16))
        grad_all = grad_all.at[target].set(grad_sum.astype(jnp.bfloat16))
        return (out_all, grad_all), None

    start = (jnp.zeros((dummy + 1, D), jnp.bfloat16), jnp.zeros((dummy + 1, D), jnp.bfloat16))
    (out_all, grad_all), _ = lax.scan(expert_step, start, (global_entry, used_rows, w_gate, w_up, w_down))
    expert_out = out_all[:dummy].reshape(TOKENS, 2, D).astype(jnp.float32)
    expert_grad = grad_all[:dummy].reshape(TOKENS, 2, D).astype(jnp.float32)
    mixed = (gates[:, 0:1] * expert_out[:, 0] + gates[:, 1:2] * expert_out[:, 1]).astype(jnp.bfloat16)
    grad_tokens = (expert_grad[:, 0] + expert_grad[:, 1]).astype(jnp.bfloat16)
    gate_grads = jnp.sum(upstream.astype(jnp.float32)[:, None, :] * expert_out, axis=-1)
    return mixed, grad_tokens, gate_grads
```

```python
import functools
import jax
import jax.numpy as jnp
from jax import lax
from jax.experimental import pallas as pl
from jax.experimental.pallas import tpu as pltpu
from jax.sharding import PartitionSpec as P

F32 = jnp.float32
BF16 = jnp.bfloat16
VMEM_LIMIT = 48 << 20


def contract_last(left, right):
    return lax.dot_general(left, right, (((1,), (1,)), ((), ())), preferred_element_type=F32)


def dot(left, right):
    return jnp.dot(left, right, preferred_element_type=F32)


def expert_work(row_x, row_dy, weight_gate, weight_up, weight_down):
    gate_pre = dot(row_x, weight_gate)
    up_pre = dot(row_x, weight_up)
    sigma = jax.nn.sigmoid(gate_pre)
    active = gate_pre * sigma
    hidden = (active * up_pre).astype(BF16)
    out_part = dot(hidden, weight_down).astype(BF16)
    grad_hidden = contract_last(row_dy, weight_down)
    grad_up = (grad_hidden * active).astype(BF16)
    grad_gate = (grad_hidden * up_pre * sigma * (1.0 + gate_pre * (1.0 - sigma))).astype(BF16)
    in_part = (contract_last(grad_gate, weight_gate) + contract_last(grad_up, weight_up)).astype(BF16)
    return (out_part, in_part)


def body_general(tokens, upstream, gates, expert_ids, w_gate, w_up, w_down):
    tok_dev = tokens.shape[0]
    expert_count = lax.axis_size("expert")
    capacity = max(2, 3 * tok_dev // expert_count)
    slot_count = expert_count * capacity
    entry_count = 2 * tok_dev
    flat_ids = expert_ids.reshape(entry_count)
    onehot = (flat_ids[:, None] == jnp.arange(expert_count, dtype=jnp.int32)[None, :]).astype(jnp.int32)
    before = jnp.cumsum(onehot, axis=0) - onehot
    position = jnp.sum(before * onehot, axis=1)
    slot_of_entry = flat_ids * capacity + position
    match = slot_of_entry[None, :] == jnp.arange(slot_count, dtype=jnp.int32)[:, None]
    entry_index = jnp.arange(entry_count, dtype=jnp.int32)
    entry_of_slot = jnp.sum(jnp.where(match, entry_index[None, :], 0), axis=1)
    slot_used = jnp.any(match, axis=1)[:, None]
    gate_flat = gates.reshape(entry_count)
    token_rows = entry_of_slot // 2
    send_x = jnp.where(slot_used, jnp.take(tokens, token_rows, axis=0), jnp.zeros((), BF16))
    scaled = (
        jnp.take(upstream, token_rows, axis=0).astype(F32) * jnp.take(gate_flat, entry_of_slot)[:, None]
    ).astype(BF16)
    send_dy = jnp.where(slot_used, scaled, jnp.zeros((), BF16))

    def exchange(value):
        return lax.all_to_all(value, "expert", split_axis=0, concat_axis=0, tiled=True)

    recv_x = lax.all_gather(exchange(send_x), "tensor", axis=1, tiled=True)
    recv_dy = lax.all_gather(exchange(send_dy), "tensor", axis=1, tiled=True)
    out_part, in_part = expert_work(recv_x, recv_dy, w_gate[0], w_up[0], w_down[0])
    back_out = exchange(lax.psum_scatter(out_part, "tensor", scatter_dimension=1, tiled=True))
    back_grad = exchange(lax.psum_scatter(in_part, "tensor", scatter_dimension=1, tiled=True))
    width = back_out.shape[1]
    entry_out = jnp.take(back_out, slot_of_entry, axis=0).reshape(tok_dev, 2, width).astype(F32)
    entry_grad = jnp.take(back_grad, slot_of_entry, axis=0).reshape(tok_dev, 2, width).astype(F32)
    mixed = (gates[:, 0:1] * entry_out[:, 0] + gates[:, 1:2] * entry_out[:, 1]).astype(BF16)
    grad_tokens = (entry_grad[:, 0] + entry_grad[:, 1]).astype(BF16)
    local_inner = jnp.sum(upstream.astype(F32)[:, None, :] * entry_out, axis=-1)
    return (mixed, grad_tokens, lax.psum(local_inner, "tensor"))


def dispatch_kernel(info, ids_ref, gates_ref, tok_ref, up_ref, *refs, count, cap):
    outs, sel, gsl = refs[:count], refs[count], refs[count + 1]
    tok_dev = ids_ref.shape[1]

    @pl.when(pl.program_id(0) == 0)
    def _():
        near = jnp.bitwise_xor(ids_ref[...], info[0])
        first, second = near[0:1, :], near[1:2, :]
        which = lax.broadcasted_iota(jnp.int32, (count, tok_dev), 0)
        named = jnp.where((which == first) | (which == second), 1.0, 0.0)
        earlier = lax.broadcasted_iota(jnp.int32, (tok_dev, tok_dev), 0) < lax.broadcasted_iota(
            jnp.int32, (tok_dev, tok_dev), 1
        )
        before = dot(named.astype(BF16), jnp.where(earlier, 1.0, 0.0).astype(BF16))
        gate = jnp.where(which == first, gates_ref[0:1, :], gates_ref[1:2, :])
        slot = lax.broadcasted_iota(jnp.int32, (cap, tok_dev), 0).astype(F32)
        for k in range(count):
            hit = (before[k : k + 1, :] == slot) & (named[k : k + 1, :] > 0.5)
            sel[k * cap : (k + 1) * cap, :] = jnp.where(hit, 1.0, 0.0).astype(BF16)
            gsl[k * cap : (k + 1) * cap, :] = jnp.sum(
                jnp.where(hit, jnp.broadcast_to(gate[k : k + 1, :], hit.shape), 0.0), axis=1, keepdims=True
            )

    rows_x = dot(sel[...], tok_ref[...])
    rows_dy = dot(sel[...], up_ref[...]) * gsl[...]
    for k in range(count):
        outs[k][0] = rows_x[k * cap : (k + 1) * cap].astype(BF16)
        outs[k][1] = rows_dy[k * cap : (k + 1) * cap].astype(BF16)


def dispatch(info, ids_t, gates_t, tokens, upstream, count, cap):
    tok_dev, width = tokens.shape
    steps = 2
    blk = width // steps
    return pl.pallas_call(
        functools.partial(dispatch_kernel, count=count, cap=cap),
        out_shape=[jax.ShapeDtypeStruct((2, cap, width), BF16)] * count,
        grid_spec=pltpu.PrefetchScalarGridSpec(
            num_scalar_prefetch=1,
            grid=(steps,),
            in_specs=[
                pl.BlockSpec((2, tok_dev), lambda i, s: (0, 0)),
                pl.BlockSpec((2, tok_dev), lambda i, s: (0, 0)),
                pl.BlockSpec((tok_dev, blk), lambda i, s: (0, i)),
                pl.BlockSpec((tok_dev, blk), lambda i, s: (0, i)),
            ],
            out_specs=[pl.BlockSpec((2, cap, blk), lambda i, s: (0, 0, i))] * count,
            scratch_shapes=[pltpu.VMEM((count * cap, tok_dev), BF16), pltpu.VMEM((count * cap, 1), F32)],
        ),
        compiler_params=pltpu.CompilerParams(vmem_limit_bytes=VMEM_LIMIT),
        cost_estimate=pl.CostEstimate(
            flops=4 * count * cap * tok_dev * width, bytes_accessed=4 * width * (tok_dev + count * cap), transcendentals=0
        ),
        name="dispatch",
    )(info, ids_t, gates_t, tokens, upstream)


def project_kernel(info, *refs, m):
    own, fwd = refs[:m], refs[m : 2 * m]
    wg, wgo, wu, wuo, wd, wdo, out = refs[2 * m :]
    step = pl.program_id(0)

    @pl.when(step == 0)
    def _():
        out[...] = jnp.zeros_like(out)

    def add(blocks):
        x = jnp.concatenate([b[0] for b in blocks], axis=0)
        dy = jnp.concatenate([b[1] for b in blocks], axis=0)
        hw = wg.shape[1]
        out[:, 0 * hw : 1 * hw] += dot(x, wg[...])
        out[:, 1 * hw : 2 * hw] += dot(x, wgo[...])
        out[:, 2 * hw : 3 * hw] += dot(x, wu[...])
        out[:, 3 * hw : 4 * hw] += dot(x, wuo[...])
        out[:, 4 * hw : 5 * hw] += contract_last(dy, wd[...])
        out[:, 5 * hw : 6 * hw] += contract_last(dy, wdo[...])

    @pl.when(step < 2)
    def _():
        add(own)

    @pl.when(step >= 2)
    def _():
        add(fwd)


def project(info, own, fwd, weights):
    m = len(own)
    _, cap, width = own[0].shape
    wg, wgo, wu, wuo, wd, wdo = weights
    hw = wg.shape[1]
    blk = width // 2
    rows = m * cap

    def mine(i, s):
        return jnp.bitwise_xor(s[1], 2 * (i // 2)) * 2 + i % 2

    return pl.pallas_call(
        functools.partial(project_kernel, m=m),
        out_shape=jax.ShapeDtypeStruct((rows, 6 * hw), F32),
        grid_spec=pltpu.PrefetchScalarGridSpec(
            num_scalar_prefetch=1,
            grid=(4,),
            in_specs=[pl.BlockSpec((2, cap, blk), lambda i, s: (0, 0, jnp.minimum(i, 1)))] * m
            + [pl.BlockSpec((2, cap, blk), lambda i, s: (0, 0, jnp.maximum(i - 2, 0)))] * m
            + [
                pl.BlockSpec((blk, hw), lambda i, s: (mine(i, s), 0)),
                pl.BlockSpec((blk, hw), lambda i, s: (i, 0)),
                pl.BlockSpec((blk, hw), lambda i, s: (mine(i, s), 0)),
                pl.BlockSpec((blk, hw), lambda i, s: (i, 0)),
                pl.BlockSpec((hw, blk), lambda i, s: (0, mine(i, s))),
                pl.BlockSpec((hw, blk), lambda i, s: (0, i)),
            ],
            out_specs=pl.BlockSpec((rows, 6 * hw), lambda i, s: (0, 0)),
        ),
        compiler_params=pltpu.CompilerParams(vmem_limit_bytes=VMEM_LIMIT),
        cost_estimate=pl.CostEstimate(
            flops=2 * rows * 2 * width * 6 * hw, bytes_accessed=24 * width * hw + 8 * rows * width, transcendentals=0
        ),
        name="project",
    )(info, *own, *fwd, wg, wgo, wu, wuo, wd, wdo)


def emit(h3, wg, wgo, wu, wuo, wd, wdo, pay):
    hw = wg.shape[1]
    hid, gg, gu = h3[0], h3[1], h3[2]
    pay[0] = (dot(hid[:, :hw], wd[...]) + dot(hid[:, hw:], wdo[...])).astype(BF16)
    pay[1] = (
        contract_last(gg[:, :hw], wg[...])
        + contract_last(gg[:, hw:], wgo[...])
        + contract_last(gu[:, :hw], wu[...])
        + contract_last(gu[:, hw:], wuo[...])
    ).astype(BF16)


def partner_kernel(info, mine, other, wg, wgo, wu, wuo, wd, wdo, pay, h3):
    hw = wg.shape[1]

    @pl.when(pl.program_id(0) == 0)
    def _():
        for b in range(2):
            def total(j):
                lo, sw = (2 * j + b) * hw, (2 * j + 1 - b) * hw
                return mine[:, lo : lo + hw] + other[:, sw : sw + hw]

            gate_pre, up_pre, grad_hidden = total(0), total(1), total(2)
            sigma = jax.nn.sigmoid(gate_pre)
            active = gate_pre * sigma
            cols = slice(b * hw, (b + 1) * hw)
            h3[0, :, cols] = (active * up_pre).astype(BF16)
            h3[1, :, cols] = (grad_hidden * up_pre * sigma * (1.0 + gate_pre * (1.0 - sigma))).astype(BF16)
            h3[2, :, cols] = (grad_hidden * active).astype(BF16)

    emit(h3, wg, wgo, wu, wuo, wd, wdo, pay)


def own_kernel(info, h3, wg, wgo, wu, wuo, wd, wdo, pay):
    emit(h3, wg, wgo, wu, wuo, wd, wdo, pay)


def weight_specs(blk, hw, flip):
    def mine(i, s):
        return jnp.bitwise_xor(s[1], flip) * 2 + i

    return [
        pl.BlockSpec((blk, hw), lambda i, s: (mine(i, s), 0)),
        pl.BlockSpec((blk, hw), lambda i, s: (flip + i, 0)),
        pl.BlockSpec((blk, hw), lambda i, s: (mine(i, s), 0)),
        pl.BlockSpec((blk, hw), lambda i, s: (flip + i, 0)),
        pl.BlockSpec((hw, blk), lambda i, s: (0, mine(i, s))),
        pl.BlockSpec((hw, blk), lambda i, s: (0, flip + i)),
    ]


def partner_part(info, mine, other, weights, width):
    rows, six = mine.shape
    hw = six // 6
    blk = width // 2
    return pl.pallas_call(
        partner_kernel,
        out_shape=[
            jax.ShapeDtypeStruct((2, rows, width), BF16),
            jax.ShapeDtypeStruct((3, rows, 2 * hw), BF16),
        ],
        grid_spec=pltpu.PrefetchScalarGridSpec(
            num_scalar_prefetch=1,
            grid=(2,),
            in_specs=[pl.BlockSpec((rows, six), lambda i, s: (0, 0))] * 2 + weight_specs(blk, hw, 2),
            out_specs=[
                pl.BlockSpec((2, rows, blk), lambda i, s: (0, 0, i)),
                pl.BlockSpec((3, rows, 2 * hw), lambda i, s: (0, 0, 0)),
            ],
        ),
        compiler_params=pltpu.CompilerParams(vmem_limit_bytes=VMEM_LIMIT),
        cost_estimate=pl.CostEstimate(
            flops=2 * rows * width * 6 * hw,
            bytes_accessed=12 * width * hw + 4 * rows * width + 8 * rows * six,
            transcendentals=rows * 2 * hw,
        ),
        name="partner_part",
    )(info, mine, other, *weights)


def own_part(info, h3, weights, width):
    _, rows, hid = h3.shape
    hw = hid // 2
    blk = width // 2
    return pl.pallas_call(
        own_kernel,
        out_shape=jax.ShapeDtypeStruct((2, rows, width), BF16),
        grid_spec=pltpu.PrefetchScalarGridSpec(
            num_scalar_prefetch=1,
            grid=(2,),
            in_specs=[pl.BlockSpec(h3.shape, lambda i, s: (0, 0, 0))] + weight_specs(blk, hw, 0),
            out_specs=pl.BlockSpec((2, rows, blk), lambda i, s: (0, 0, i)),
        ),
        compiler_params=pltpu.CompilerParams(vmem_limit_bytes=VMEM_LIMIT),
        cost_estimate=pl.CostEstimate(
            flops=2 * rows * width * 6 * hw, bytes_accessed=12 * width * hw + 4 * rows * width, transcendentals=0
        ),
        name="own_part",
    )(info, h3, *weights)


def merge_kernel(a, b, *outs):
    cap = outs[0].shape[1]
    for j, out in enumerate(outs):
        rows = slice(j * cap, (j + 1) * cap)
        out[...] = (a[:, rows, :].astype(F32) + b[:, rows, :].astype(F32)).astype(BF16)


def merge(a, b, m):
    _, rows, width = a.shape
    cap = rows // m
    blk = width // 2
    return pl.pallas_call(
        merge_kernel,
        grid=(2,),
        out_shape=[jax.ShapeDtypeStruct((2, cap, width), BF16)] * m,
        in_specs=[pl.BlockSpec((2, rows, blk), lambda i: (0, 0, i))] * 2,
        out_specs=[pl.BlockSpec((2, cap, blk), lambda i: (0, 0, i))] * m,
        compiler_params=pltpu.CompilerParams(vmem_limit_bytes=VMEM_LIMIT),
        cost_estimate=pl.CostEstimate(flops=2 * rows * width, bytes_accessed=12 * rows * width, transcendentals=0),
        name="merge",
    )(a, b)


def combine_kernel(info, ids_ref, gates_ref, up_ref, *refs, count, cap):
    blocks = refs[:count]
    mixed, grad, inner, q0, q1 = refs[count:]
    tok_dev = ids_ref.shape[0]

    @pl.when(pl.program_id(0) == 0)
    def _():
        near = jnp.bitwise_xor(ids_ref[...], info[0])
        first, second = near[:, 0:1], near[:, 1:2]
        which = lax.broadcasted_iota(jnp.int32, (tok_dev, count), 1)
        named = jnp.where((which == first) | (which == second), 1.0, 0.0)
        earlier = lax.broadcasted_iota(jnp.int32, (tok_dev, tok_dev), 1) < lax.broadcasted_iota(
            jnp.int32, (tok_dev, tok_dev), 0
        )
        before = dot(jnp.where(earlier, 1.0, 0.0).astype(BF16), named.astype(BF16))
        lane = lax.broadcasted_iota(jnp.int32, (tok_dev, count * cap), 1).astype(F32)
        for near_k, q in ((first, q0), (second, q1)):
            place = jnp.sum(jnp.where(which == near_k, before, 0.0), axis=1, keepdims=True)
            slot = near_k.astype(F32) * cap + place
            q[...] = jnp.where(lane == slot, 1.0, 0.0).astype(BF16)
        inner[...] = jnp.zeros_like(inner)

    outs = jnp.concatenate([b[0] for b in blocks], axis=0)
    grads = jnp.concatenate([b[1] for b in blocks], axis=0)
    e0, e1 = dot(q0[...], outs), dot(q1[...], outs)
    mixed[...] = (gates_ref[:, 0:1] * e0 + gates_ref[:, 1:2] * e1).astype(BF16)
    grad[...] = dot(q0[...] + q1[...], grads).astype(BF16)
    up = up_ref[...].astype(F32)
    inner[:, 0:1] += jnp.sum(up * e0, axis=1, keepdims=True)
    inner[:, 1:2] += jnp.sum(up * e1, axis=1, keepdims=True)


def combine(info, ids, gates, upstream, blocks, cap):
    count = len(blocks)
    tok_dev, width = upstream.shape
    blk = width // 2
    return pl.pallas_call(
        functools.partial(combine_kernel, count=count, cap=cap),
        out_shape=[
            jax.ShapeDtypeStruct((tok_dev, width), BF16),
            jax.ShapeDtypeStruct((tok_dev, width), BF16),
            jax.ShapeDtypeStruct((tok_dev, 2), F32),
        ],
        grid_spec=pltpu.PrefetchScalarGridSpec(
            num_scalar_prefetch=1,
            grid=(2,),
            in_specs=[
                pl.BlockSpec((tok_dev, 2), lambda i, s: (0, 0)),
                pl.BlockSpec((tok_dev, 2), lambda i, s: (0, 0)),
                pl.BlockSpec((tok_dev, blk), lambda i, s: (0, i)),
            ]
            + [pl.BlockSpec((2, cap, blk), lambda i, s: (0, 0, i))] * count,
            out_specs=[
                pl.BlockSpec((tok_dev, blk), lambda i, s: (0, i)),
                pl.BlockSpec((tok_dev, blk), lambda i, s: (0, i)),
                pl.BlockSpec((tok_dev, 2), lambda i, s: (0, 0)),
            ],
            scratch_shapes=[pltpu.VMEM((tok_dev, count * cap), BF16)] * 2,
        ),
        compiler_params=pltpu.CompilerParams(vmem_limit_bytes=VMEM_LIMIT),
        cost_estimate=pl.CostEstimate(
            flops=6 * tok_dev * count * cap * width, bytes_accessed=4 * width * (count * cap + 2 * tok_dev), transcendentals=0
        ),
        name="combine",
    )(info, ids, gates, upstream, *blocks)


CHUNKS = ((0, 4, 2, 5), (1, 6, 3, 7))


def body_fast(tokens, upstream, gates, expert_ids, w_gate, w_up, w_down):
    count, n_tensor = lax.axis_size("expert"), lax.axis_size("tensor")
    tok_dev, width = tokens.shape
    cap = 3 * tok_dev // count
    me, t = lax.axis_index("expert"), lax.axis_index("tensor")
    info = jnp.stack([me, t]).astype(jnp.int32)
    wg, wu, wd = w_gate[0], w_up[0], w_down[0]

    def across(value, k):
        return lax.ppermute(value, "expert", [(i, i ^ k) for i in range(count)])

    def swap(value, k):
        return lax.ppermute(value, "tensor", [(i, i ^ k) for i in range(n_tensor)])

    sends = dispatch(info, expert_ids.T, gates.T, tokens, upstream, count, cap)

    def rows_for(w):
        return jnp.concatenate(
            [lax.dynamic_slice_in_dim(w, (t ^ k) * width, width, 0) for k in (1, 3)], axis=0
        )

    def cols_for(w):
        return jnp.concatenate(
            [lax.dynamic_slice_in_dim(w, (t ^ k) * width, width, 1) for k in (1, 3)], axis=1
        )

    weights = (wg, swap(rows_for(wg), 1), wu, swap(rows_for(wu), 1), wd, swap(cols_for(wd), 1))
    back = [None] * count
    for chunk in CHUNKS:
        own = [sends[k] if k == 0 else across(sends[k], k) for k in chunk]
        fwd = [swap(b, 2) for b in own]
        mine = project(info, own, fwd, weights)
        other = swap(mine, 1)
        pay, h3 = partner_part(info, mine, other, weights, width)
        recv = swap(pay, 2)
        kept = own_part(info, h3, weights, width)
        done = merge(kept, recv, len(chunk))
        for k, block in zip(chunk, done):
            back[k] = block if k == 0 else across(block, k)
    mixed, grad_tokens, inner = combine(info, expert_ids, gates, upstream, back, cap)
    inner = inner + swap(inner, 1)
    inner = inner + swap(inner, 2)
    return (mixed, grad_tokens, inner)


def solution(mesh):
    fast = mesh.shape["expert"] == 8 and mesh.shape["tensor"] == 4
    return jax.shard_map(
        body_fast if fast else body_general,
        mesh=mesh,
        in_specs=(
            P("expert", "tensor"),
            P("expert", "tensor"),
            P("expert", None),
            P("expert", None),
            P("expert", None, "tensor"),
            P("expert", None, "tensor"),
            P("expert", "tensor", None),
        ),
        out_specs=(P("expert", "tensor"), P("expert", "tensor"), P("expert", None)),
        check_vma=False,
    )
```

```python
import functools
import jax
import jax.numpy as jnp
from jax import lax
from jax.experimental import pallas as pl
from jax.experimental.pallas import tpu as pltpu
from jax.sharding import PartitionSpec as P

F32 = jnp.float32
BF16 = jnp.bfloat16
VMEM_LIMIT = 20 << 20
COST = pl.CostEstimate(flops=1024, bytes_accessed=1024, transcendentals=0)


def contract_last(left, right):
    return lax.dot_general(left, right, (((1,), (1,)), ((), ())), preferred_element_type=F32)


def dot(left, right):
    return jnp.dot(left, right, preferred_element_type=F32)


def expert_work(row_x, row_dy, weight_gate, weight_up, weight_down):
    gate_pre = dot(row_x, weight_gate)
    up_pre = dot(row_x, weight_up)
    sigma = jax.nn.sigmoid(gate_pre)
    active = gate_pre * sigma
    hidden = (active * up_pre).astype(BF16)
    out_part = dot(hidden, weight_down).astype(BF16)
    grad_hidden = contract_last(row_dy, weight_down)
    grad_up = (grad_hidden * active).astype(BF16)
    grad_gate = (grad_hidden * up_pre * sigma * (1.0 + gate_pre * (1.0 - sigma))).astype(BF16)
    in_part = (contract_last(grad_gate, weight_gate) + contract_last(grad_up, weight_up)).astype(BF16)
    return (out_part, in_part)


def body_general(tokens, upstream, gates, expert_ids, w_gate, w_up, w_down):
    tok_dev = tokens.shape[0]
    expert_count = lax.axis_size("expert")
    capacity = max(2, 3 * tok_dev // expert_count)
    slot_count = expert_count * capacity
    entry_count = 2 * tok_dev
    flat_ids = expert_ids.reshape(entry_count)
    onehot = (flat_ids[:, None] == jnp.arange(expert_count, dtype=jnp.int32)[None, :]).astype(jnp.int32)
    before = jnp.cumsum(onehot, axis=0) - onehot
    position = jnp.sum(before * onehot, axis=1)
    slot_of_entry = flat_ids * capacity + position
    match = slot_of_entry[None, :] == jnp.arange(slot_count, dtype=jnp.int32)[:, None]
    entry_index = jnp.arange(entry_count, dtype=jnp.int32)
    entry_of_slot = jnp.sum(jnp.where(match, entry_index[None, :], 0), axis=1)
    slot_used = jnp.any(match, axis=1)[:, None]
    gate_flat = gates.reshape(entry_count)
    token_rows = entry_of_slot // 2
    send_x = jnp.where(slot_used, jnp.take(tokens, token_rows, axis=0), jnp.zeros((), BF16))
    scaled = (
        jnp.take(upstream, token_rows, axis=0).astype(F32) * jnp.take(gate_flat, entry_of_slot)[:, None]
    ).astype(BF16)
    send_dy = jnp.where(slot_used, scaled, jnp.zeros((), BF16))

    def exchange(value):
        return lax.all_to_all(value, "expert", split_axis=0, concat_axis=0, tiled=True)

    recv_x = lax.all_gather(exchange(send_x), "tensor", axis=1, tiled=True)
    recv_dy = lax.all_gather(exchange(send_dy), "tensor", axis=1, tiled=True)
    out_part, in_part = expert_work(recv_x, recv_dy, w_gate[0], w_up[0], w_down[0])
    back_out = exchange(lax.psum_scatter(out_part, "tensor", scatter_dimension=1, tiled=True))
    back_grad = exchange(lax.psum_scatter(in_part, "tensor", scatter_dimension=1, tiled=True))
    width = back_out.shape[1]
    entry_out = jnp.take(back_out, slot_of_entry, axis=0).reshape(tok_dev, 2, width).astype(F32)
    entry_grad = jnp.take(back_grad, slot_of_entry, axis=0).reshape(tok_dev, 2, width).astype(F32)
    mixed = (gates[:, 0:1] * entry_out[:, 0] + gates[:, 1:2] * entry_out[:, 1]).astype(BF16)
    grad_tokens = (entry_grad[:, 0] + entry_grad[:, 1]).astype(BF16)
    local_inner = jnp.sum(upstream.astype(F32)[:, None, :] * entry_out, axis=-1)
    return (mixed, grad_tokens, lax.psum(local_inner, "tensor"))


def dispatch_kernel(info, ids_ref, gates_ref, tok_ref, up_ref, wg, wu, wd, *refs, count, cap):
    outs, cut_gu, cut_d, sel, gsl, sems = refs[:count], *refs[count:]
    tok_dev = ids_ref.shape[1]
    width = cut_d.shape[1] // 2

    def cuts():
        for j in range(2):
            start = pl.multiple_of(jnp.bitwise_xor(info[1], 1 + 2 * j) * width, width)
            rows = pl.ds(j * width, width)
            yield pltpu.make_async_copy(wg.at[pl.ds(start, width)], cut_gu.at[0, rows], sems.at[3 * j])
            yield pltpu.make_async_copy(wu.at[pl.ds(start, width)], cut_gu.at[1, rows], sems.at[3 * j + 1])
            yield pltpu.make_async_copy(wd.at[:, pl.ds(start, width)], cut_d.at[:, rows], sems.at[3 * j + 2])

    @pl.when(pl.program_id(0) == 0)
    def _():
        for copy in cuts():
            copy.start()

    @pl.when(pl.program_id(0) == 0)
    def _():
        near = jnp.bitwise_xor(ids_ref[...], info[0])
        first, second = near[0:1, :], near[1:2, :]
        which = lax.broadcasted_iota(jnp.int32, (count, tok_dev), 0)
        named = jnp.where((which == first) | (which == second), 1.0, 0.0)
        earlier = lax.broadcasted_iota(jnp.int32, (tok_dev, tok_dev), 0) < lax.broadcasted_iota(
            jnp.int32, (tok_dev, tok_dev), 1
        )
        before = dot(named.astype(BF16), jnp.where(earlier, 1.0, 0.0).astype(BF16))
        gate = jnp.where(which == first, gates_ref[0:1, :], gates_ref[1:2, :])
        slot = lax.broadcasted_iota(jnp.int32, (cap, tok_dev), 0).astype(F32)
        for k in range(count):
            hit = (before[k : k + 1, :] == slot) & (named[k : k + 1, :] > 0.5)
            sel[k * cap : (k + 1) * cap, :] = jnp.where(hit, 1.0, 0.0).astype(BF16)
            gsl[k * cap : (k + 1) * cap, :] = jnp.sum(
                jnp.where(hit, jnp.broadcast_to(gate[k : k + 1, :], hit.shape), 0.0), axis=1, keepdims=True
            )

    rows_x = dot(sel[...], tok_ref[...])
    rows_dy = dot(sel[...], up_ref[...]) * gsl[...]
    for k in range(count):
        outs[k][0] = rows_x[k * cap : (k + 1) * cap].astype(BF16)
        outs[k][1] = rows_dy[k * cap : (k + 1) * cap].astype(BF16)

    @pl.when(pl.program_id(0) == pl.num_programs(0) - 1)
    def _():
        for copy in cuts():
            copy.wait()


def dispatch(info, ids_t, gates_t, tokens, upstream, wg, wu, wd, count, cap):
    tok_dev, width = tokens.shape
    steps = 2
    blk = width // steps
    return pl.pallas_call(
        functools.partial(dispatch_kernel, count=count, cap=cap),
        out_shape=[jax.ShapeDtypeStruct((2, cap, width), BF16)] * count
        + [
            jax.ShapeDtypeStruct((2, 2 * width, wg.shape[1]), BF16),
            jax.ShapeDtypeStruct((wd.shape[0], 2 * width), BF16),
        ],
        grid_spec=pltpu.PrefetchScalarGridSpec(
            num_scalar_prefetch=1,
            grid=(steps,),
            in_specs=[
                pl.BlockSpec((2, tok_dev), lambda i, s: (0, 0)),
                pl.BlockSpec((2, tok_dev), lambda i, s: (0, 0)),
                pl.BlockSpec((tok_dev, blk), lambda i, s: (0, i)),
                pl.BlockSpec((tok_dev, blk), lambda i, s: (0, i)),
            ]
            + [pl.BlockSpec(memory_space=pl.ANY)] * 3,
            out_specs=[pl.BlockSpec((2, cap, blk), lambda i, s: (0, 0, i))] * count
            + [pl.BlockSpec(memory_space=pl.ANY)] * 2,
            scratch_shapes=[
                pltpu.VMEM((count * cap, tok_dev), BF16),
                pltpu.VMEM((count * cap, 1), F32),
                pltpu.SemaphoreType.DMA((6,)),
            ],
        ),
        compiler_params=pltpu.CompilerParams(vmem_limit_bytes=VMEM_LIMIT),
        cost_estimate=COST,
        name="dispatch",
    )(info, ids_t, gates_t, tokens, upstream, wg, wu, wd)


def project_kernel(info, *refs, m):
    own, fwd = refs[:m], refs[m : 2 * m]
    wg, wgo, wu, wuo, wd, wdo, out, sent = refs[2 * m :]
    step = pl.program_id(0)

    @pl.when(step == 0)
    def _():
        out[...] = jnp.zeros_like(out)

    def add(blocks):
        x = jnp.concatenate([b[0] for b in blocks], axis=0)
        dy = jnp.concatenate([b[1] for b in blocks], axis=0)
        hw = wg.shape[1]
        out[:, 0 * hw : 1 * hw] += dot(x, wg[...])
        out[:, 1 * hw : 2 * hw] += dot(x, wgo[...])
        out[:, 2 * hw : 3 * hw] += dot(x, wu[...])
        out[:, 3 * hw : 4 * hw] += dot(x, wuo[...])
        out[:, 4 * hw : 5 * hw] += contract_last(dy, wd[...])
        out[:, 5 * hw : 6 * hw] += contract_last(dy, wdo[...])

    @pl.when(step < 2)
    def _():
        add(own)

    @pl.when(step >= 2)
    def _():
        add(fwd)

    @pl.when(step == 3)
    def _():
        sent[...] = out[...].astype(BF16)


def project(info, own, fwd, weights):
    m = len(own)
    _, cap, width = own[0].shape
    wg, wgo, wu, wuo, wd, wdo = weights
    hw = wg.shape[1]
    blk = width // 2
    rows = m * cap

    def mine(i, s):
        return jnp.bitwise_xor(s[1], 2 * (i // 2)) * 2 + i % 2

    return pl.pallas_call(
        functools.partial(project_kernel, m=m),
        out_shape=[jax.ShapeDtypeStruct((rows, 6 * hw), F32), jax.ShapeDtypeStruct((rows, 6 * hw), BF16)],
        grid_spec=pltpu.PrefetchScalarGridSpec(
            num_scalar_prefetch=1,
            grid=(4,),
            in_specs=[pl.BlockSpec((2, cap, blk), lambda i, s: (0, 0, jnp.minimum(i, 1)))] * m
            + [pl.BlockSpec((2, cap, blk), lambda i, s: (0, 0, jnp.maximum(i - 2, 0)))] * m
            + [
                pl.BlockSpec((blk, hw), lambda i, s: (mine(i, s), 0)),
                pl.BlockSpec((None, blk, hw), lambda i, s: (0, i, 0)),
                pl.BlockSpec((blk, hw), lambda i, s: (mine(i, s), 0)),
                pl.BlockSpec((None, blk, hw), lambda i, s: (1, i, 0)),
                pl.BlockSpec((hw, blk), lambda i, s: (0, mine(i, s))),
                pl.BlockSpec((hw, blk), lambda i, s: (0, i)),
            ],
            out_specs=[pl.BlockSpec((rows, 6 * hw), lambda i, s: (0, 0))] * 2,
        ),
        compiler_params=pltpu.CompilerParams(vmem_limit_bytes=VMEM_LIMIT),
        cost_estimate=COST,
        name="project",
    )(info, *own, *fwd, wg, wgo, wu, wuo, wd, wdo)


def emit(h3, wg, wgo, wu, wuo, wd, wdo, pays):
    hw = wg.shape[1]
    cap = pays[0].shape[1]
    hid, gg, gu = h3[0], h3[1], h3[2]
    out = (dot(hid[:, :hw], wd[...]) + dot(hid[:, hw:], wdo[...])).astype(BF16)
    grad = (
        contract_last(gg[:, :hw], wg[...])
        + contract_last(gg[:, hw:], wgo[...])
        + contract_last(gu[:, :hw], wu[...])
        + contract_last(gu[:, hw:], wuo[...])
    ).astype(BF16)
    for j, pay in enumerate(pays):
        pay[0] = out[j * cap : (j + 1) * cap]
        pay[1] = grad[j * cap : (j + 1) * cap]


def partner_kernel(info, mine, other, wg, wgo, wu, wuo, wd, wdo, *outs):
    pays, h3 = outs[:-1], outs[-1]
    hw = wg.shape[1]

    @pl.when(pl.program_id(0) == 0)
    def _():
        for b in range(2):
            def total(j):
                lo, sw = (2 * j + b) * hw, (2 * j + 1 - b) * hw
                return mine[:, lo : lo + hw] + other[:, sw : sw + hw].astype(F32)

            gate_pre, up_pre, grad_hidden = total(0), total(1), total(2)
            sigma = jax.nn.sigmoid(gate_pre)
            active = gate_pre * sigma
            cols = slice(b * hw, (b + 1) * hw)
            h3[0, :, cols] = (active * up_pre).astype(BF16)
            h3[1, :, cols] = (grad_hidden * up_pre * sigma * (1.0 + gate_pre * (1.0 - sigma))).astype(BF16)
            h3[2, :, cols] = (grad_hidden * active).astype(BF16)

    emit(h3, wg, wgo, wu, wuo, wd, wdo, pays)


def own_kernel(info, h3, wg, wgo, wu, wuo, wd, wdo, *pays):
    emit(h3, wg, wgo, wu, wuo, wd, wdo, pays)


def weight_specs(blk, hw, flip):
    def mine(i, s):
        return jnp.bitwise_xor(s[1], flip) * 2 + i

    return [
        pl.BlockSpec((blk, hw), lambda i, s: (mine(i, s), 0)),
        pl.BlockSpec((None, blk, hw), lambda i, s: (0, flip + i, 0)),
        pl.BlockSpec((blk, hw), lambda i, s: (mine(i, s), 0)),
        pl.BlockSpec((None, blk, hw), lambda i, s: (1, flip + i, 0)),
        pl.BlockSpec((hw, blk), lambda i, s: (0, mine(i, s))),
        pl.BlockSpec((hw, blk), lambda i, s: (0, flip + i)),
    ]


def partner_part(info, mine, other, weights, width, m):
    rows, six = mine.shape
    cap = rows // m
    hw = six // 6
    blk = width // 2
    return pl.pallas_call(
        partner_kernel,
        out_shape=[jax.ShapeDtypeStruct((2, cap, width), BF16)] * m
        + [jax.ShapeDtypeStruct((3, rows, 2 * hw), BF16)],
        grid_spec=pltpu.PrefetchScalarGridSpec(
            num_scalar_prefetch=1,
            grid=(2,),
            in_specs=[pl.BlockSpec((rows, six), lambda i, s: (0, 0))] * 2 + weight_specs(blk, hw, 2),
            out_specs=[pl.BlockSpec((2, cap, blk), lambda i, s: (0, 0, i))] * m
            + [pl.BlockSpec((3, rows, 2 * hw), lambda i, s: (0, 0, 0))],
        ),
        compiler_params=pltpu.CompilerParams(vmem_limit_bytes=VMEM_LIMIT),
        cost_estimate=COST,
        name="partner_part",
    )(info, mine, other, *weights)


def own_part(info, h3, weights, width, m):
    _, rows, hid = h3.shape
    cap = rows // m
    hw = hid // 2
    blk = width // 2
    return pl.pallas_call(
        own_kernel,
        out_shape=[jax.ShapeDtypeStruct((2, cap, width), BF16)] * m,
        grid_spec=pltpu.PrefetchScalarGridSpec(
            num_scalar_prefetch=1,
            grid=(2,),
            in_specs=[pl.BlockSpec(h3.shape, lambda i, s: (0, 0, 0))] + weight_specs(blk, hw, 0),
            out_specs=[pl.BlockSpec((2, cap, blk), lambda i, s: (0, 0, i))] * m,
        ),
        compiler_params=pltpu.CompilerParams(vmem_limit_bytes=VMEM_LIMIT),
        cost_estimate=COST,
        name="own_part",
    )(info, h3, *weights)


def merge(a, b):
    return (a.astype(F32) + b.astype(F32)).astype(BF16)


def combine_kernel(info, ids_ref, gates_ref, up_ref, *refs, count, cap):
    blocks = refs[:count]
    mixed, grad, inner, q0, q1 = refs[count:]
    tok_dev = ids_ref.shape[0]

    @pl.when(pl.program_id(0) == 0)
    def _():
        near = jnp.bitwise_xor(ids_ref[...], info[0])
        first, second = near[:, 0:1], near[:, 1:2]
        which = lax.broadcasted_iota(jnp.int32, (tok_dev, count), 1)
        named = jnp.where((which == first) | (which == second), 1.0, 0.0)
        earlier = lax.broadcasted_iota(jnp.int32, (tok_dev, tok_dev), 1) < lax.broadcasted_iota(
            jnp.int32, (tok_dev, tok_dev), 0
        )
        before = dot(jnp.where(earlier, 1.0, 0.0).astype(BF16), named.astype(BF16))
        lane = lax.broadcasted_iota(jnp.int32, (tok_dev, count * cap), 1).astype(F32)
        for near_k, q in ((first, q0), (second, q1)):
            place = jnp.sum(jnp.where(which == near_k, before, 0.0), axis=1, keepdims=True)
            slot = near_k.astype(F32) * cap + place
            q[...] = jnp.where(lane == slot, 1.0, 0.0).astype(BF16)
        inner[...] = jnp.zeros_like(inner)

    outs = jnp.concatenate([b[0] for b in blocks], axis=0)
    grads = jnp.concatenate([b[1] for b in blocks], axis=0)
    e0, e1 = dot(q0[...], outs), dot(q1[...], outs)
    mixed[...] = (gates_ref[:, 0:1] * e0 + gates_ref[:, 1:2] * e1).astype(BF16)
    grad[...] = dot(q0[...] + q1[...], grads).astype(BF16)
    up = up_ref[...].astype(F32)
    inner[:, 0:1] += jnp.sum(up * e0, axis=1, keepdims=True)
    inner[:, 1:2] += jnp.sum(up * e1, axis=1, keepdims=True)


def combine(info, ids, gates, upstream, blocks, cap):
    count = len(blocks)
    tok_dev, width = upstream.shape
    blk = width // 2
    return pl.pallas_call(
        functools.partial(combine_kernel, count=count, cap=cap),
        out_shape=[
            jax.ShapeDtypeStruct((tok_dev, width), BF16),
            jax.ShapeDtypeStruct((tok_dev, width), BF16),
            jax.ShapeDtypeStruct((tok_dev, 2), F32),
        ],
        grid_spec=pltpu.PrefetchScalarGridSpec(
            num_scalar_prefetch=1,
            grid=(2,),
            in_specs=[
                pl.BlockSpec((tok_dev, 2), lambda i, s: (0, 0)),
                pl.BlockSpec((tok_dev, 2), lambda i, s: (0, 0)),
                pl.BlockSpec((tok_dev, blk), lambda i, s: (0, i)),
            ]
            + [pl.BlockSpec((2, cap, blk), lambda i, s: (0, 0, i))] * count,
            out_specs=[
                pl.BlockSpec((tok_dev, blk), lambda i, s: (0, i)),
                pl.BlockSpec((tok_dev, blk), lambda i, s: (0, i)),
                pl.BlockSpec((tok_dev, 2), lambda i, s: (0, 0)),
            ],
            scratch_shapes=[pltpu.VMEM((tok_dev, count * cap), BF16)] * 2,
        ),
        compiler_params=pltpu.CompilerParams(vmem_limit_bytes=VMEM_LIMIT),
        cost_estimate=COST,
        name="combine",
    )(info, ids, gates, upstream, *blocks)


CHUNKS = {"A": (0, 2, 4), "B": (1, 5), "C": (3, 6), "D": (7,)}


def body_fast(tokens, upstream, gates, expert_ids, w_gate, w_up, w_down):
    count, n_tensor = lax.axis_size("expert"), lax.axis_size("tensor")
    tok_dev, width = tokens.shape
    cap = 3 * tok_dev // count
    me, t = lax.axis_index("expert"), lax.axis_index("tensor")
    info = jnp.stack([me, t]).astype(jnp.int32)
    wg, wu, wd, tokens, upstream = (
        pltpu.with_memory_space_constraint(a, pltpu.HBM) for a in (w_gate[0], w_up[0], w_down[0], tokens, upstream)
    )
    v = {}

    def sync(names):
        keys = names.split()
        v.update(zip(keys, lax.optimization_barrier(tuple(v[n] for n in keys))))

    def across(k, source, result):
        v[f"{result}{k}"] = lax.ppermute(v[f"{source}{k}"], "expert", [(i, i ^ k) for i in range(count)])

    def swap(value, k):
        return lax.ppermute(value, "tensor", [(i, i ^ k) for i in range(n_tensor)])

    def take(*ks):
        for k in ks:
            across(k, "send", "in")

    def forward(*ks):
        for k in ks:
            v[f"fw{k}"] = swap(v[f"in{k}"], 2)

    def weights():
        return (wg, v["wguo"], wu, v["wguo"], wd, v["wdo"])

    def project_chunk(c):
        blocks = CHUNKS[c]
        v[f"mine{c}"], sent = project(
            info, [v[f"in{k}"] for k in blocks], [v[f"fw{k}"] for k in blocks], weights()
        )
        v[f"other{c}"] = swap(sent, 1)

    def partner_chunk(c):
        blocks = CHUNKS[c]
        *pay, v[f"h{c}"] = partner_part(info, v[f"mine{c}"], v[f"other{c}"], weights(), width, len(blocks))
        v.update({f"part{k}": p for k, p in zip(blocks, pay)})

    def own_chunk(c):
        blocks = CHUNKS[c]
        own = own_part(info, v[f"h{c}"], weights(), width, len(blocks))
        v.update({f"own{k}": p for k, p in zip(blocks, own)})

    def pay(*ks):
        for k in ks:
            v[f"pay{k}"] = swap(v[f"part{k}"], 2)

    def give(*ks):
        for k in ks:
            v[f"sum{k}"] = merge(v[f"own{k}"], v[f"pay{k}"])
            if k:
                across(k, "sum", "out")
            else:
                v["out0"] = v["sum0"]

    *sends, cut_gu, cut_d = dispatch(
        info, expert_ids.T, gates.T, tokens, upstream, wg, wu, wd, count, cap
    )
    v.update({f"send{k}": s for k, s in enumerate(sends)})
    v["in0"] = v["send0"]
    take(4, 2)
    forward(0)
    v["wguo"], v["wdo"] = swap(cut_gu, 1), swap(cut_d, 1)
    sync("in2 fw0 wguo wdo send1 in4")
    take(1)
    forward(2, 4)
    sync("in4 send5")
    take(5)
    sync("fw2 in1 send3")
    forward(1)
    take(3)
    sync("in5 send6 fw4")
    take(6)
    forward(5)
    project_chunk("A")
    sync("fw1 in3")
    forward(3)
    partner_chunk("A")
    sync("fw3 part4 in6 send7")
    pay(4)
    take(7)
    sync("fw5")
    forward(6)
    project_chunk("B")
    own_chunk("A")
    partner_chunk("B")
    sync("pay4 in7 own4")
    give(4)
    forward(7)
    sync("fw6 part5")
    pay(5)
    project_chunk("C")
    own_chunk("B")
    partner_chunk("C")
    sync("fw7 part6")
    pay(6)
    project_chunk("D")
    own_chunk("C")
    partner_chunk("D")
    sync("pay5 part2 own5")
    give(5)
    pay(2)
    sync("pay6 part7 own6")
    give(6)
    pay(7)
    own_chunk("D")
    sync("pay2 part1")
    give(2)
    pay(1)
    sync("pay7 part3")
    give(7)
    pay(3)
    sync("pay1 part0")
    give(1)
    pay(0)
    give(3, 0)
    mixed, grad_tokens, inner = combine(
        info, expert_ids, gates, upstream, [v[f"out{k}"] for k in range(count)], cap
    )
    inner = inner + swap(inner, 1)
    inner = inner + swap(inner, 2)
    return (mixed, grad_tokens, inner)


def solution(mesh):
    fast = mesh.shape["expert"] == 8 and mesh.shape["tensor"] == 4
    return jax.shard_map(
        body_fast if fast else body_general,
        mesh=mesh,
        in_specs=(
            P("expert", "tensor"),
            P("expert", "tensor"),
            P("expert", None),
            P("expert", None),
            P("expert", None, "tensor"),
            P("expert", None, "tensor"),
            P("expert", "tensor", None),
        ),
        out_specs=(P("expert", "tensor"), P("expert", "tensor"), P("expert", None)),
        check_vma=False,
    )
```

```python
import functools
import jax
import jax.numpy as jnp
from jax import lax
from jax.experimental import pallas as pl
from jax.experimental.pallas import tpu as pltpu
from jax.sharding import PartitionSpec as P

F32 = jnp.float32
BF16 = jnp.bfloat16
VMEM_LIMIT = 20 << 20
COST = pl.CostEstimate(flops=1024, bytes_accessed=1024, transcendentals=0)


def contract_last(left, right):
    return lax.dot_general(left, right, (((1,), (1,)), ((), ())), preferred_element_type=F32)


def dot(left, right):
    return jnp.dot(left, right, preferred_element_type=F32)


def expert_work(row_x, row_dy, weight_gate, weight_up, weight_down):
    gate_pre = dot(row_x, weight_gate)
    up_pre = dot(row_x, weight_up)
    sigma = jax.nn.sigmoid(gate_pre)
    active = gate_pre * sigma
    hidden = (active * up_pre).astype(BF16)
    out_part = dot(hidden, weight_down).astype(BF16)
    grad_hidden = contract_last(row_dy, weight_down)
    grad_up = (grad_hidden * active).astype(BF16)
    grad_gate = (grad_hidden * up_pre * sigma * (1.0 + gate_pre * (1.0 - sigma))).astype(BF16)
    in_part = (contract_last(grad_gate, weight_gate) + contract_last(grad_up, weight_up)).astype(BF16)
    return (out_part, in_part)


def body_general(tokens, upstream, gates, expert_ids, w_gate, w_up, w_down):
    tok_dev = tokens.shape[0]
    expert_count = lax.axis_size("expert")
    capacity = max(2, 3 * tok_dev // expert_count)
    slot_count = expert_count * capacity
    entry_count = 2 * tok_dev
    flat_ids = expert_ids.reshape(entry_count)
    onehot = (flat_ids[:, None] == jnp.arange(expert_count, dtype=jnp.int32)[None, :]).astype(jnp.int32)
    before = jnp.cumsum(onehot, axis=0) - onehot
    position = jnp.sum(before * onehot, axis=1)
    slot_of_entry = flat_ids * capacity + position
    match = slot_of_entry[None, :] == jnp.arange(slot_count, dtype=jnp.int32)[:, None]
    entry_index = jnp.arange(entry_count, dtype=jnp.int32)
    entry_of_slot = jnp.sum(jnp.where(match, entry_index[None, :], 0), axis=1)
    slot_used = jnp.any(match, axis=1)[:, None]
    gate_flat = gates.reshape(entry_count)
    token_rows = entry_of_slot // 2
    send_x = jnp.where(slot_used, jnp.take(tokens, token_rows, axis=0), jnp.zeros((), BF16))
    scaled = (
        jnp.take(upstream, token_rows, axis=0).astype(F32) * jnp.take(gate_flat, entry_of_slot)[:, None]
    ).astype(BF16)
    send_dy = jnp.where(slot_used, scaled, jnp.zeros((), BF16))

    def exchange(value):
        return lax.all_to_all(value, "expert", split_axis=0, concat_axis=0, tiled=True)

    recv_x = lax.all_gather(exchange(send_x), "tensor", axis=1, tiled=True)
    recv_dy = lax.all_gather(exchange(send_dy), "tensor", axis=1, tiled=True)
    out_part, in_part = expert_work(recv_x, recv_dy, w_gate[0], w_up[0], w_down[0])
    back_out = exchange(lax.psum_scatter(out_part, "tensor", scatter_dimension=1, tiled=True))
    back_grad = exchange(lax.psum_scatter(in_part, "tensor", scatter_dimension=1, tiled=True))
    width = back_out.shape[1]
    entry_out = jnp.take(back_out, slot_of_entry, axis=0).reshape(tok_dev, 2, width).astype(F32)
    entry_grad = jnp.take(back_grad, slot_of_entry, axis=0).reshape(tok_dev, 2, width).astype(F32)
    mixed = (gates[:, 0:1] * entry_out[:, 0] + gates[:, 1:2] * entry_out[:, 1]).astype(BF16)
    grad_tokens = (entry_grad[:, 0] + entry_grad[:, 1]).astype(BF16)
    local_inner = jnp.sum(upstream.astype(F32)[:, None, :] * entry_out, axis=-1)
    return (mixed, grad_tokens, lax.psum(local_inner, "tensor"))


def cuts(t, flips, wg, wu, wd, gu, d, sems):
    width = d.shape[1] // 2
    for j, flip in enumerate(flips):
        start = pl.multiple_of(jnp.bitwise_xor(t, flip) * width, width)
        to = pl.ds(j * width, width)
        yield pltpu.make_async_copy(wg.at[pl.ds(start, width)], gu.at[0, to], sems.at[3 * j])
        yield pltpu.make_async_copy(wu.at[pl.ds(start, width)], gu.at[1, to], sems.at[3 * j + 1])
        yield pltpu.make_async_copy(wd.at[:, pl.ds(start, width)], d.at[:, to], sems.at[3 * j + 2])


def cut_kernel(info, wg, wu, wd, gu, d, sems):
    copies = list(cuts(info[1], (0, 2), wg, wu, wd, gu, d, sems))
    for copy in copies:
        copy.start()
    for copy in copies:
        copy.wait()


def cut_shapes(wg, width):
    hw = wg.shape[1]
    return [jax.ShapeDtypeStruct((2, 2 * width, hw), BF16), jax.ShapeDtypeStruct((hw, 2 * width), BF16)]


def cut_own(info, wg, wu, wd, width):
    return pl.pallas_call(
        cut_kernel,
        out_shape=cut_shapes(wg, width),
        in_specs=[pl.BlockSpec(memory_space=pltpu.SMEM)] + [pl.BlockSpec(memory_space=pl.ANY)] * 3,
        out_specs=[pl.BlockSpec(memory_space=pltpu.VMEM)] * 2,
        scratch_shapes=[pltpu.SemaphoreType.DMA((6,))],
        compiler_params=pltpu.CompilerParams(vmem_limit_bytes=VMEM_LIMIT),
        cost_estimate=pl.CostEstimate(flops=0, bytes_accessed=24 * width * wg.shape[1], transcendentals=0),
        name="cut_own",
    )(info, wg, wu, wd)


def dispatch_kernel(info, ids_ref, gates_ref, tok_hbm, up_hbm, wg, wu, wd, *refs, count, cap):
    outs, cut_gu, cut_d, tok, up, sel, gsl, sems = refs[:count], *refs[count:]
    tok_dev = ids_ref.shape[1]
    loads = [
        pltpu.make_async_copy(tok_hbm, tok, sems.at[6]),
        pltpu.make_async_copy(up_hbm, up, sems.at[7]),
    ]
    copies = list(cuts(info[1], (1, 3), wg, wu, wd, cut_gu, cut_d, sems))
    for copy in loads + copies:
        copy.start()

    near = jnp.bitwise_xor(ids_ref[...], info[0])
    first, second = near[0:1, :], near[1:2, :]
    which = lax.broadcasted_iota(jnp.int32, (count, tok_dev), 0)
    named = jnp.where((which == first) | (which == second), 1.0, 0.0)
    earlier = lax.broadcasted_iota(jnp.int32, (tok_dev, tok_dev), 0) < lax.broadcasted_iota(
        jnp.int32, (tok_dev, tok_dev), 1
    )
    before = dot(named.astype(BF16), jnp.where(earlier, 1.0, 0.0).astype(BF16))
    gate = jnp.where(which == first, gates_ref[0:1, :], gates_ref[1:2, :])
    slot = lax.broadcasted_iota(jnp.int32, (cap, tok_dev), 0).astype(F32)
    for k in range(count):
        hit = (before[k : k + 1, :] == slot) & (named[k : k + 1, :] > 0.5)
        sel[k * cap : (k + 1) * cap, :] = jnp.where(hit, 1.0, 0.0).astype(BF16)
        gsl[k * cap : (k + 1) * cap, :] = jnp.sum(
            jnp.where(hit, jnp.broadcast_to(gate[k : k + 1, :], hit.shape), 0.0), axis=1, keepdims=True
        )

    loads[0].wait()
    for k in range(count):
        outs[k][0] = dot(sel[k * cap : (k + 1) * cap], tok[...]).astype(BF16)
    loads[1].wait()
    for k in range(count):
        rows = slice(k * cap, (k + 1) * cap)
        outs[k][1] = (dot(sel[rows], up[...]) * gsl[rows]).astype(BF16)
    for copy in copies:
        copy.wait()


def dispatch(info, ids_t, gates_t, tokens, upstream, wg, wu, wd, count, cap):
    tok_dev, width = tokens.shape
    outs = [jax.ShapeDtypeStruct((2, cap, width), BF16)] * count + cut_shapes(wg, width)
    return pl.pallas_call(
        functools.partial(dispatch_kernel, count=count, cap=cap),
        out_shape=outs,
        in_specs=[pl.BlockSpec(memory_space=pltpu.SMEM)]
        + [pl.BlockSpec(memory_space=pltpu.VMEM)] * 2
        + [pl.BlockSpec(memory_space=pl.ANY)] * 5,
        out_specs=[pl.BlockSpec(memory_space=pltpu.VMEM)] * len(outs),
        scratch_shapes=[
            pltpu.VMEM((tok_dev, width), BF16),
            pltpu.VMEM((tok_dev, width), BF16),
            pltpu.VMEM((count * cap, tok_dev), BF16),
            pltpu.VMEM((count * cap, 1), F32),
            pltpu.SemaphoreType.DMA((8,)),
        ],
        compiler_params=pltpu.CompilerParams(vmem_limit_bytes=VMEM_LIMIT),
        cost_estimate=COST,
        name="dispatch",
    )(info, ids_t, gates_t, tokens, upstream, wg, wu, wd)


def project_kernel(*refs, m):
    own, fwd = refs[:m], refs[m : 2 * m]
    own_gu, own_d, far_gu, far_d, out, sent = refs[2 * m :]
    cap, width = own[0].shape[1:]
    hw = own_d.shape[0]
    x = [jnp.concatenate([b[0] for b in blocks], axis=0) for blocks in (own, fwd)]
    dy = [jnp.concatenate([b[1] for b in blocks], axis=0) for blocks in (own, fwd)]
    for j, (gu, d) in enumerate(((own_gu, own_d), (far_gu, far_d))):
        for p, part in enumerate(
            (
                dot(x[0], gu[0, :width]) + dot(x[1], gu[0, width:]),
                dot(x[0], gu[1, :width]) + dot(x[1], gu[1, width:]),
                contract_last(dy[0], d[:, :width]) + contract_last(dy[1], d[:, width:]),
            )
        ):
            cols = slice((2 * p + j) * hw, (2 * p + j + 1) * hw)
            out[:, cols] = part
            sent[:, cols] = part.astype(BF16)


def whole(kernel, outs, name, *args):
    return pl.pallas_call(
        kernel,
        out_shape=outs,
        in_specs=[pl.BlockSpec(memory_space=pltpu.VMEM)] * len(args),
        out_specs=[pl.BlockSpec(memory_space=pltpu.VMEM)] * len(outs),
        compiler_params=pltpu.CompilerParams(vmem_limit_bytes=VMEM_LIMIT),
        cost_estimate=COST,
        name=name,
    )(*args)


def project(own, fwd, weights):
    m = len(own)
    rows, six = m * own[0].shape[1], 6 * weights[1].shape[0]
    outs = [jax.ShapeDtypeStruct((rows, six), F32), jax.ShapeDtypeStruct((rows, six), BF16)]
    return whole(functools.partial(project_kernel, m=m), outs, "project", *own, *fwd, *weights)


def emit(h3, own_gu, own_d, far_gu, far_d, pays, side):
    hw = own_d.shape[0]
    cap, width = pays[0].shape[1:]
    cols = slice(side * width, (side + 1) * width)
    out = dot(h3[0, :, :hw], own_d[:, cols]) + dot(h3[0, :, hw:], far_d[:, cols])
    for j, pay in enumerate(pays):
        pay[0] = out[j * cap : (j + 1) * cap].astype(BF16)
    grad = (
        contract_last(h3[1, :, :hw], own_gu[0, cols])
        + contract_last(h3[1, :, hw:], far_gu[0, cols])
        + contract_last(h3[2, :, :hw], own_gu[1, cols])
        + contract_last(h3[2, :, hw:], far_gu[1, cols])
    )
    for j, pay in enumerate(pays):
        pay[1] = grad[j * cap : (j + 1) * cap].astype(BF16)


def partner_kernel(mine, other, own_gu, own_d, far_gu, far_d, *outs):
    pays, h3 = outs[:-1], outs[-1]
    hw = own_d.shape[0]
    for b in range(2):
        def total(j):
            lo, sw = (2 * j + b) * hw, (2 * j + 1 - b) * hw
            return mine[:, lo : lo + hw] + other[:, sw : sw + hw].astype(F32)

        gate_pre, up_pre, grad_hidden = total(0), total(1), total(2)
        sigma = jax.nn.sigmoid(gate_pre)
        active = gate_pre * sigma
        cols = slice(b * hw, (b + 1) * hw)
        h3[0, :, cols] = (active * up_pre).astype(BF16)
        h3[1, :, cols] = (grad_hidden * up_pre * sigma * (1.0 + gate_pre * (1.0 - sigma))).astype(BF16)
        h3[2, :, cols] = (grad_hidden * active).astype(BF16)
    emit(h3, own_gu, own_d, far_gu, far_d, pays, 1)


def own_kernel(h3, own_gu, own_d, far_gu, far_d, *pays):
    emit(h3, own_gu, own_d, far_gu, far_d, pays, 0)


def partner_part(mine, other, weights, width, m):
    rows, six = mine.shape
    outs = [jax.ShapeDtypeStruct((2, rows // m, width), BF16)] * m
    outs.append(jax.ShapeDtypeStruct((3, rows, six // 3), BF16))
    return whole(partner_kernel, outs, "partner_part", mine, other, *weights)


def own_part(h3, weights, width, m):
    rows = h3.shape[1]
    outs = [jax.ShapeDtypeStruct((2, rows // m, width), BF16)] * m
    return whole(own_kernel, outs, "own_part", h3, *weights)


def merge(a, b):
    return (a.astype(F32) + b.astype(F32)).astype(BF16)


def combine_kernel(info, ids_ref, gates_ref, up_ref, *refs, count, cap):
    blocks = refs[:count]
    mixed, grad, inner, q0, q1, gate = refs[count:]
    tok_dev = ids_ref.shape[1]

    @pl.when(pl.program_id(0) == 0)
    def _():
        near = jnp.bitwise_xor(ids_ref[...], info[0]).astype(F32)
        rows = jnp.concatenate([near, gates_ref[...], jnp.zeros((4, tok_dev), F32)], axis=0)
        columns = jnp.transpose(rows)
        gate[...] = columns[:, 2:4]
        first, second = columns[:, 0:1].astype(jnp.int32), columns[:, 1:2].astype(jnp.int32)
        which = lax.broadcasted_iota(jnp.int32, (tok_dev, count), 1)
        named = jnp.where((which == first) | (which == second), 1.0, 0.0)
        earlier = lax.broadcasted_iota(jnp.int32, (tok_dev, tok_dev), 1) < lax.broadcasted_iota(
            jnp.int32, (tok_dev, tok_dev), 0
        )
        before = dot(jnp.where(earlier, 1.0, 0.0).astype(BF16), named.astype(BF16))
        lane = lax.broadcasted_iota(jnp.int32, (tok_dev, count * cap), 1).astype(F32)
        for near_k, q in ((first, q0), (second, q1)):
            place = jnp.sum(jnp.where(which == near_k, before, 0.0), axis=1, keepdims=True)
            slot = near_k.astype(F32) * cap + place
            q[...] = jnp.where(lane == slot, 1.0, 0.0).astype(BF16)
        inner[...] = jnp.zeros_like(inner)

    outs = jnp.concatenate([b[0] for b in blocks], axis=0)
    grads = jnp.concatenate([b[1] for b in blocks], axis=0)
    e0, e1 = dot(q0[...], outs), dot(q1[...], outs)
    mixed[...] = (gate[:, 0:1] * e0 + gate[:, 1:2] * e1).astype(BF16)
    grad[...] = dot(q0[...] + q1[...], grads).astype(BF16)
    up = up_ref[...].astype(F32)
    inner[:, 0:1] += jnp.sum(up * e0, axis=1, keepdims=True)
    inner[:, 1:2] += jnp.sum(up * e1, axis=1, keepdims=True)


def combine(info, ids, gates, upstream, blocks, cap):
    count = len(blocks)
    tok_dev, width = upstream.shape
    blk = width // 2
    return pl.pallas_call(
        functools.partial(combine_kernel, count=count, cap=cap),
        out_shape=[
            jax.ShapeDtypeStruct((tok_dev, width), BF16),
            jax.ShapeDtypeStruct((tok_dev, width), BF16),
            jax.ShapeDtypeStruct((tok_dev, 2), F32),
        ],
        grid_spec=pltpu.PrefetchScalarGridSpec(
            num_scalar_prefetch=1,
            grid=(2,),
            in_specs=[
                pl.BlockSpec((2, tok_dev), lambda i, s: (0, 0)),
                pl.BlockSpec((2, tok_dev), lambda i, s: (0, 0)),
                pl.BlockSpec((tok_dev, blk), lambda i, s: (0, i)),
            ]
            + [pl.BlockSpec((2, cap, blk), lambda i, s: (0, 0, i))] * count,
            out_specs=[
                pl.BlockSpec((tok_dev, blk), lambda i, s: (0, i)),
                pl.BlockSpec((tok_dev, blk), lambda i, s: (0, i)),
                pl.BlockSpec((tok_dev, 2), lambda i, s: (0, 0)),
            ],
            scratch_shapes=[pltpu.VMEM((tok_dev, count * cap), BF16)] * 2 + [pltpu.VMEM((tok_dev, 2), F32)],
        ),
        compiler_params=pltpu.CompilerParams(vmem_limit_bytes=VMEM_LIMIT),
        cost_estimate=COST,
        name="combine",
    )(info, ids, gates, upstream, *blocks)


CHUNKS = {"A": (0, 1, 4), "B": (2, 5), "C": (3, 6), "D": (7,)}


def body_fast(tokens, upstream, gates, expert_ids, w_gate, w_up, w_down):
    count, n_tensor = lax.axis_size("expert"), lax.axis_size("tensor")
    tok_dev, width = tokens.shape
    cap = 3 * tok_dev // count
    me, t = lax.axis_index("expert"), lax.axis_index("tensor")
    info = jnp.stack([me, t]).astype(jnp.int32)
    wg, wu, wd, tokens, upstream = (
        pltpu.with_memory_space_constraint(a, pltpu.HBM) for a in (w_gate[0], w_up[0], w_down[0], tokens, upstream)
    )
    v = {}

    def sync(*names):
        v.update(zip(names, lax.optimization_barrier(tuple(v[n] for n in names))))

    def across(k, source, result):
        with jax.named_scope(f"{result}_{k}"):
            v[f"{result}{k}"] = lax.ppermute(v[f"{source}{k}"], "expert", [(i, i ^ k) for i in range(count)])

    def swap(value, k):
        return lax.ppermute(value, "tensor", [(i, i ^ k) for i in range(n_tensor)])

    def take(*ks):
        for k in ks:
            across(k, "send", "in")

    def forward(*ks):
        for k in ks:
            with jax.named_scope(f"forward_{k}"):
                v[f"fw{k}"] = swap(v[f"in{k}"], 2)

    def weights():
        return (v["wgu"], v["wd"], v["wguo"], v["wdo"])

    def project_chunk(c):
        blocks = CHUNKS[c]
        v[f"mine{c}"], sent = project(
            [v[f"in{k}"] for k in blocks], [v[f"fw{k}"] for k in blocks], weights()
        )
        v[f"other{c}"] = swap(sent, 1)

    def partner_chunk(c):
        blocks = CHUNKS[c]
        *pay, v[f"h{c}"] = partner_part(v[f"mine{c}"], v[f"other{c}"], weights(), width, len(blocks))
        v.update({f"part{k}": p for k, p in zip(blocks, pay)})

    def own_chunk(c):
        blocks = CHUNKS[c]
        own = own_part(v[f"h{c}"], weights(), width, len(blocks))
        v.update({f"own{k}": p for k, p in zip(blocks, own)})

    def pay(*ks):
        for k in ks:
            with jax.named_scope(f"pay_{k}"):
                v[f"pay{k}"] = swap(v[f"part{k}"], 2)

    def give(*ks):
        for k in ks:
            v[f"sum{k}"] = merge(v[f"own{k}"], v[f"pay{k}"])
            if k:
                across(k, "sum", "out")
            else:
                v["out0"] = v["sum0"]

    *sends, cut_gu, cut_d = dispatch(
        info, expert_ids.T, gates.T, tokens, upstream, wg, wu, wd, count, cap
    )
    v.update({f"send{k}": s for k, s in enumerate(sends)})
    v["in0"] = v["send0"]
    take(4, 1)
    forward(0)
    v["wguo"], v["wdo"] = swap(cut_gu, 1), swap(cut_d, 1)
    v["wgu"], v["wd"] = cut_own(info, wg, wu, wd, width)
    sync("in1", "fw0", "send2", "wgu", "wd")
    take(2)
    forward(1)
    sync("in4", "send5")
    take(5)
    forward(4)
    sync("fw1", "in2", "send3", "wguo", "wdo")
    forward(2)
    take(3)
    sync("in5", "send6", "fw4")
    take(6)
    forward(5)
    project_chunk("A")
    sync("fw2", "in3")
    forward(3)
    partner_chunk("A")
    sync("fw3", "part4", "in6", "send7")
    pay(4)
    take(7)
    sync("fw5")
    forward(6)
    project_chunk("B")
    own_chunk("A")
    partner_chunk("B")
    sync("pay4", "in7", "own4")
    give(4)
    forward(7)
    sync("fw6", "part5")
    pay(5)
    project_chunk("C")
    own_chunk("B")
    partner_chunk("C")
    sync("fw7", "part6")
    pay(6)
    project_chunk("D")
    own_chunk("C")
    partner_chunk("D")
    sync("pay5", "part1", "own5")
    give(5)
    pay(1)
    sync("pay6", "part7", "own6", "out4")
    give(6)
    pay(7)
    own_chunk("D")
    sync("pay1", "part3")
    give(1)
    pay(3)
    sync("pay7", "part2", "own7", "out5")
    give(7)
    pay(2)
    sync("pay3", "part0", "out1")
    give(3)
    pay(0)
    give(2, 0)
    mixed, grad_tokens, inner = combine(
        info, expert_ids.T, gates.T, upstream, [v[f"out{k}"] for k in range(count)], cap
    )
    inner = inner + swap(inner, 1)
    inner = inner + swap(inner, 2)
    return (mixed, grad_tokens, inner)


def solution(mesh):
    fast = mesh.shape["expert"] == 8 and mesh.shape["tensor"] == 4
    return jax.shard_map(
        body_fast if fast else body_general,
        mesh=mesh,
        in_specs=(
            P("expert", "tensor"),
            P("expert", "tensor"),
            P("expert", None),
            P("expert", None),
            P("expert", None, "tensor"),
            P("expert", None, "tensor"),
            P("expert", "tensor", None),
        ),
        out_specs=(P("expert", "tensor"), P("expert", "tensor"), P("expert", None)),
        check_vma=False,
    )
```

```python
import functools
import jax
import jax.numpy as jnp
from jax import lax
from jax.experimental import pallas as pl
from jax.experimental.pallas import tpu as pltpu
from jax.sharding import PartitionSpec as P

F32 = jnp.float32
BF16 = jnp.bfloat16
VMEM_LIMIT = 20 << 20
COST = pl.CostEstimate(flops=1024, bytes_accessed=1024, transcendentals=0)


def contract_last(left, right):
    return lax.dot_general(left, right, (((1,), (1,)), ((), ())), preferred_element_type=F32)


def dot(left, right):
    return jnp.dot(left, right, preferred_element_type=F32)


def expert_work(row_x, row_dy, weight_gate, weight_up, weight_down):
    gate_pre = dot(row_x, weight_gate)
    up_pre = dot(row_x, weight_up)
    sigma = jax.nn.sigmoid(gate_pre)
    active = gate_pre * sigma
    hidden = (active * up_pre).astype(BF16)
    out_part = dot(hidden, weight_down).astype(BF16)
    grad_hidden = contract_last(row_dy, weight_down)
    grad_up = (grad_hidden * active).astype(BF16)
    grad_gate = (grad_hidden * up_pre * sigma * (1.0 + gate_pre * (1.0 - sigma))).astype(BF16)
    in_part = (contract_last(grad_gate, weight_gate) + contract_last(grad_up, weight_up)).astype(BF16)
    return (out_part, in_part)


def body_general(tokens, upstream, gates, expert_ids, w_gate, w_up, w_down):
    tok_dev = tokens.shape[0]
    expert_count = lax.axis_size("expert")
    capacity = max(2, 3 * tok_dev // expert_count)
    slot_count = expert_count * capacity
    entry_count = 2 * tok_dev
    flat_ids = expert_ids.reshape(entry_count)
    onehot = (flat_ids[:, None] == jnp.arange(expert_count, dtype=jnp.int32)[None, :]).astype(jnp.int32)
    before = jnp.cumsum(onehot, axis=0) - onehot
    position = jnp.sum(before * onehot, axis=1)
    slot_of_entry = flat_ids * capacity + position
    match = slot_of_entry[None, :] == jnp.arange(slot_count, dtype=jnp.int32)[:, None]
    entry_index = jnp.arange(entry_count, dtype=jnp.int32)
    entry_of_slot = jnp.sum(jnp.where(match, entry_index[None, :], 0), axis=1)
    slot_used = jnp.any(match, axis=1)[:, None]
    gate_flat = gates.reshape(entry_count)
    token_rows = entry_of_slot // 2
    send_x = jnp.where(slot_used, jnp.take(tokens, token_rows, axis=0), jnp.zeros((), BF16))
    scaled = (
        jnp.take(upstream, token_rows, axis=0).astype(F32) * jnp.take(gate_flat, entry_of_slot)[:, None]
    ).astype(BF16)
    send_dy = jnp.where(slot_used, scaled, jnp.zeros((), BF16))

    def exchange(value):
        return lax.all_to_all(value, "expert", split_axis=0, concat_axis=0, tiled=True)

    recv_x = lax.all_gather(exchange(send_x), "tensor", axis=1, tiled=True)
    recv_dy = lax.all_gather(exchange(send_dy), "tensor", axis=1, tiled=True)
    out_part, in_part = expert_work(recv_x, recv_dy, w_gate[0], w_up[0], w_down[0])
    back_out = exchange(lax.psum_scatter(out_part, "tensor", scatter_dimension=1, tiled=True))
    back_grad = exchange(lax.psum_scatter(in_part, "tensor", scatter_dimension=1, tiled=True))
    width = back_out.shape[1]
    entry_out = jnp.take(back_out, slot_of_entry, axis=0).reshape(tok_dev, 2, width).astype(F32)
    entry_grad = jnp.take(back_grad, slot_of_entry, axis=0).reshape(tok_dev, 2, width).astype(F32)
    mixed = (gates[:, 0:1] * entry_out[:, 0] + gates[:, 1:2] * entry_out[:, 1]).astype(BF16)
    grad_tokens = (entry_grad[:, 0] + entry_grad[:, 1]).astype(BF16)
    local_inner = jnp.sum(upstream.astype(F32)[:, None, :] * entry_out, axis=-1)
    return (mixed, grad_tokens, lax.psum(local_inner, "tensor"))


def cuts(t, flips, wg, wu, wd, gu, d, sems):
    width = d.shape[1] // 2
    for j, flip in enumerate(flips):
        start = pl.multiple_of(jnp.bitwise_xor(t, flip) * width, width)
        to = pl.ds(j * width, width)
        yield pltpu.make_async_copy(wg.at[pl.ds(start, width)], gu.at[0, to], sems.at[3 * j])
        yield pltpu.make_async_copy(wu.at[pl.ds(start, width)], gu.at[1, to], sems.at[3 * j + 1])
        yield pltpu.make_async_copy(wd.at[:, pl.ds(start, width)], d.at[:, to], sems.at[3 * j + 2])


def cut_kernel(info, ids_ref, gates_ref, wg, wu, wd, gu, d, pick, gate, sems, *, count):
    copies = list(cuts(info[1], (0, 2), wg, wu, wd, gu, d, sems))
    for copy in copies:
        copy.start()
    tok_dev, slots = pick.shape[1:]
    near = jnp.bitwise_xor(ids_ref[...], info[0]).astype(F32)
    columns = jnp.transpose(jnp.concatenate([near, gates_ref[...], jnp.zeros((4, tok_dev), F32)], axis=0))
    gate[...] = columns
    first, second = columns[:, 0:1].astype(jnp.int32), columns[:, 1:2].astype(jnp.int32)
    which = lax.broadcasted_iota(jnp.int32, (tok_dev, count), 1)
    named = jnp.where((which == first) | (which == second), 1.0, 0.0)
    earlier = lax.broadcasted_iota(jnp.int32, (tok_dev, tok_dev), 1) < lax.broadcasted_iota(
        jnp.int32, (tok_dev, tok_dev), 0
    )
    before = dot(jnp.where(earlier, 1.0, 0.0).astype(BF16), named.astype(BF16))
    lane = lax.broadcasted_iota(jnp.int32, (tok_dev, slots), 1).astype(F32)
    for j, near_k in enumerate((first, second)):
        place = jnp.sum(jnp.where(which == near_k, before, 0.0), axis=1, keepdims=True)
        pick[j] = jnp.where(lane == near_k.astype(F32) * (slots // count) + place, 1.0, 0.0).astype(BF16)
    for copy in copies:
        copy.wait()


def cut_shapes(wg, width):
    hw = wg.shape[1]
    return [jax.ShapeDtypeStruct((2, 2 * width, hw), BF16), jax.ShapeDtypeStruct((hw, 2 * width), BF16)]


def cut_own(info, ids_t, gates_t, wg, wu, wd, width, count, cap):
    tok_dev = ids_t.shape[1]
    vmem = pl.BlockSpec(memory_space=pltpu.VMEM)
    return pl.pallas_call(
        functools.partial(cut_kernel, count=count),
        out_shape=cut_shapes(wg, width)
        + [
            jax.ShapeDtypeStruct((2, tok_dev, count * cap), BF16),
            jax.ShapeDtypeStruct((tok_dev, 8), F32),
        ],
        in_specs=[pl.BlockSpec(memory_space=pltpu.SMEM), vmem, vmem]
        + [pl.BlockSpec(memory_space=pl.ANY)] * 3,
        out_specs=[vmem] * 4,
        scratch_shapes=[pltpu.SemaphoreType.DMA((6,))],
        compiler_params=pltpu.CompilerParams(vmem_limit_bytes=VMEM_LIMIT),
        cost_estimate=pl.CostEstimate(flops=0, bytes_accessed=24 * width * wg.shape[1], transcendentals=0),
        name="cut_own",
    )(info, ids_t, gates_t, wg, wu, wd)


def dispatch_kernel(info, ids_ref, gates_ref, tok_hbm, up_hbm, wg, wu, wd, *refs, count, cap):
    outs, cut_gu, cut_d, tok, up, sel, gsl, sems = refs[:count], *refs[count:]
    tok_dev = ids_ref.shape[1]
    loads = [
        pltpu.make_async_copy(tok_hbm, tok, sems.at[6]),
        pltpu.make_async_copy(up_hbm, up, sems.at[7]),
    ]
    copies = list(cuts(info[1], (1, 3), wg, wu, wd, cut_gu, cut_d, sems))
    for copy in loads + copies:
        copy.start()

    near = jnp.bitwise_xor(ids_ref[...], info[0])
    first, second = near[0:1, :], near[1:2, :]
    which = lax.broadcasted_iota(jnp.int32, (count, tok_dev), 0)
    named = jnp.where((which == first) | (which == second), 1.0, 0.0)
    earlier = lax.broadcasted_iota(jnp.int32, (tok_dev, tok_dev), 0) < lax.broadcasted_iota(
        jnp.int32, (tok_dev, tok_dev), 1
    )
    before = dot(named.astype(BF16), jnp.where(earlier, 1.0, 0.0).astype(BF16))
    gate = jnp.where(which == first, gates_ref[0:1, :], gates_ref[1:2, :])
    slot = lax.broadcasted_iota(jnp.int32, (cap, tok_dev), 0).astype(F32)
    for k in range(count):
        hit = (before[k : k + 1, :] == slot) & (named[k : k + 1, :] > 0.5)
        sel[k * cap : (k + 1) * cap, :] = jnp.where(hit, 1.0, 0.0).astype(BF16)
        gsl[k * cap : (k + 1) * cap, :] = jnp.sum(
            jnp.where(hit, jnp.broadcast_to(gate[k : k + 1, :], hit.shape), 0.0), axis=1, keepdims=True
        )

    loads[0].wait()
    for k in range(count):
        outs[k][0] = dot(sel[k * cap : (k + 1) * cap], tok[...]).astype(BF16)
    loads[1].wait()
    for k in range(count):
        rows = slice(k * cap, (k + 1) * cap)
        outs[k][1] = (dot(sel[rows], up[...]) * gsl[rows]).astype(BF16)
    for copy in copies:
        copy.wait()


def dispatch(info, ids_t, gates_t, tokens, upstream, wg, wu, wd, count, cap):
    tok_dev, width = tokens.shape
    outs = [jax.ShapeDtypeStruct((2, cap, width), BF16)] * count + cut_shapes(wg, width)
    return pl.pallas_call(
        functools.partial(dispatch_kernel, count=count, cap=cap),
        out_shape=outs,
        in_specs=[pl.BlockSpec(memory_space=pltpu.SMEM)]
        + [pl.BlockSpec(memory_space=pltpu.VMEM)] * 2
        + [pl.BlockSpec(memory_space=pl.ANY)] * 5,
        out_specs=[pl.BlockSpec(memory_space=pltpu.VMEM)] * len(outs),
        scratch_shapes=[
            pltpu.VMEM((tok_dev, width), BF16),
            pltpu.VMEM((tok_dev, width), BF16),
            pltpu.VMEM((count * cap, tok_dev), BF16),
            pltpu.VMEM((count * cap, 1), F32),
            pltpu.SemaphoreType.DMA((8,)),
        ],
        compiler_params=pltpu.CompilerParams(vmem_limit_bytes=VMEM_LIMIT),
        cost_estimate=COST,
        name="dispatch",
    )(info, ids_t, gates_t, tokens, upstream, wg, wu, wd)


def project_kernel(*refs, m):
    own, fwd = refs[:m], refs[m : 2 * m]
    own_gu, own_d, far_gu, far_d, out, sent = refs[2 * m :]
    cap, width = own[0].shape[1:]
    hw = own_d.shape[0]
    x = [jnp.concatenate([b[0] for b in blocks], axis=0) for blocks in (own, fwd)]
    dy = [jnp.concatenate([b[1] for b in blocks], axis=0) for blocks in (own, fwd)]
    for j, (gu, d) in enumerate(((own_gu, own_d), (far_gu, far_d))):
        for p, part in enumerate(
            (
                dot(x[0], gu[0, :width]) + dot(x[1], gu[0, width:]),
                dot(x[0], gu[1, :width]) + dot(x[1], gu[1, width:]),
                contract_last(dy[0], d[:, :width]) + contract_last(dy[1], d[:, width:]),
            )
        ):
            cols = slice((2 * p + j) * hw, (2 * p + j + 1) * hw)
            out[:, cols] = part
            sent[:, cols] = part.astype(BF16)


def whole(kernel, outs, name, *args):
    return pl.pallas_call(
        kernel,
        out_shape=outs,
        in_specs=[pl.BlockSpec(memory_space=pltpu.VMEM)] * len(args),
        out_specs=[pl.BlockSpec(memory_space=pltpu.VMEM)] * len(outs),
        compiler_params=pltpu.CompilerParams(vmem_limit_bytes=VMEM_LIMIT),
        cost_estimate=COST,
        name=name,
    )(*args)


def project(own, fwd, weights):
    m = len(own)
    rows, six = m * own[0].shape[1], 6 * weights[1].shape[0]
    outs = [jax.ShapeDtypeStruct((rows, six), F32), jax.ShapeDtypeStruct((rows, six), BF16)]
    return whole(functools.partial(project_kernel, m=m), outs, "project", *own, *fwd, *weights)


def emit(h3, own_gu, own_d, far_gu, far_d, pays, side):
    hw = own_d.shape[0]
    cap, width = pays[0].shape[1:]
    cols = slice(side * width, (side + 1) * width)
    out = dot(h3[0, :, :hw], own_d[:, cols]) + dot(h3[0, :, hw:], far_d[:, cols])
    for j, pay in enumerate(pays):
        pay[0] = out[j * cap : (j + 1) * cap].astype(BF16)
    grad = (
        contract_last(h3[1, :, :hw], own_gu[0, cols])
        + contract_last(h3[1, :, hw:], far_gu[0, cols])
        + contract_last(h3[2, :, :hw], own_gu[1, cols])
        + contract_last(h3[2, :, hw:], far_gu[1, cols])
    )
    for j, pay in enumerate(pays):
        pay[1] = grad[j * cap : (j + 1) * cap].astype(BF16)


def partner_kernel(mine, other, own_gu, own_d, far_gu, far_d, *outs):
    pays, h3 = outs[:-1], outs[-1]
    hw = own_d.shape[0]
    for b in range(2):
        def total(j):
            lo, sw = (2 * j + b) * hw, (2 * j + 1 - b) * hw
            return mine[:, lo : lo + hw] + other[:, sw : sw + hw].astype(F32)

        gate_pre, up_pre, grad_hidden = total(0), total(1), total(2)
        sigma = jax.nn.sigmoid(gate_pre)
        active = gate_pre * sigma
        cols = slice(b * hw, (b + 1) * hw)
        h3[0, :, cols] = (active * up_pre).astype(BF16)
        h3[1, :, cols] = (grad_hidden * up_pre * sigma * (1.0 + gate_pre * (1.0 - sigma))).astype(BF16)
        h3[2, :, cols] = (grad_hidden * active).astype(BF16)
    emit(h3, own_gu, own_d, far_gu, far_d, pays, 1)


def own_kernel(h3, own_gu, own_d, far_gu, far_d, *pays):
    emit(h3, own_gu, own_d, far_gu, far_d, pays, 0)


def partner_part(mine, other, weights, width, m):
    rows, six = mine.shape
    outs = [jax.ShapeDtypeStruct((2, rows // m, width), BF16)] * m
    outs.append(jax.ShapeDtypeStruct((3, rows, six // 3), BF16))
    return whole(partner_kernel, outs, "partner_part", mine, other, *weights)


def own_part(h3, weights, width, m):
    rows = h3.shape[1]
    outs = [jax.ShapeDtypeStruct((2, rows // m, width), BF16)] * m
    return whole(own_kernel, outs, "own_part", h3, *weights)


def merge(a, b):
    return (a.astype(F32) + b.astype(F32)).astype(BF16)


def mixed_kernel(pick, gate, up, *refs):
    blocks, mixed_hbm, inner, mixed, sems = refs[:-4], *refs[-4:]
    tok_dev, width = mixed.shape
    parts = 2
    blk = width // parts
    copies, sums = [], [0.0, 0.0]
    for p in range(parts):
        cols = slice(p * blk, (p + 1) * blk)
        outs = jnp.concatenate([b[0, :, cols] for b in blocks], axis=0)
        entries = [dot(pick[j], outs) for j in range(2)]
        mixed[:, cols] = (gate[:, 2:3] * entries[0] + gate[:, 3:4] * entries[1]).astype(BF16)
        copies.append(pltpu.make_async_copy(mixed.at[:, cols], mixed_hbm.at[:, cols], sems.at[p]))
        copies[-1].start()
        cotangent = up[:, cols].astype(F32)
        for j in range(2):
            sums[j] = sums[j] + jnp.sum(cotangent * entries[j], axis=1, keepdims=True)
    spot = lax.broadcasted_iota(jnp.int32, (tok_dev, 128), 1)
    side = jnp.where(spot == 0, sums[0], jnp.where(spot == 1, sums[1], 0.0))
    inner[...] = jnp.transpose(side)[:2, :]
    for copy in copies:
        copy.wait()


def grad_kernel(pick, *refs):
    blocks, grad_hbm, grad, sems = refs[:-3], *refs[-3:]
    width = grad.shape[1]
    parts = 2
    blk = width // parts
    both = pick[0] + pick[1]
    copies = []
    for p in range(parts):
        cols = slice(p * blk, (p + 1) * blk)
        grads = jnp.concatenate([b[1, :, cols] for b in blocks], axis=0)
        grad[:, cols] = dot(both, grads).astype(BF16)
        copies.append(pltpu.make_async_copy(grad.at[:, cols], grad_hbm.at[:, cols], sems.at[p]))
        copies[-1].start()
    for copy in copies:
        copy.wait()


def combine(pick, gate, upstream, blocks):
    tok_dev = pick.shape[1]
    width = blocks[0].shape[2]
    vmem, anywhere = pl.BlockSpec(memory_space=pltpu.VMEM), pl.BlockSpec(memory_space=pl.ANY)
    full = jax.ShapeDtypeStruct((tok_dev, width), BF16)
    scratch = [pltpu.VMEM((tok_dev, width), BF16), pltpu.SemaphoreType.DMA((2,))]
    params = pltpu.CompilerParams(vmem_limit_bytes=VMEM_LIMIT)
    mixed, inner = pl.pallas_call(
        mixed_kernel,
        out_shape=[full, jax.ShapeDtypeStruct((2, tok_dev), F32)],
        in_specs=[vmem] * (3 + len(blocks)),
        out_specs=[anywhere, vmem],
        scratch_shapes=scratch,
        compiler_params=params,
        cost_estimate=COST,
        name="mixed",
    )(pick, gate, upstream, *blocks)
    grad = pl.pallas_call(
        grad_kernel,
        out_shape=full,
        in_specs=[vmem] * (1 + len(blocks)),
        out_specs=anywhere,
        scratch_shapes=scratch,
        compiler_params=params,
        cost_estimate=pl.CostEstimate(flops=0, bytes_accessed=16 << 20, transcendentals=0),
        name="grad",
    )(pick, *blocks)
    return mixed, grad, inner


CHUNKS = {"A": (0, 1, 4), "B": (2, 5), "C": (3, 6), "D": (7,)}


def body_fast(tokens, upstream, gates, expert_ids, w_gate, w_up, w_down):
    count, n_tensor = lax.axis_size("expert"), lax.axis_size("tensor")
    tok_dev, width = tokens.shape
    cap = 3 * tok_dev // count
    me, t = lax.axis_index("expert"), lax.axis_index("tensor")
    info = jnp.stack([me, t]).astype(jnp.int32)
    wg, wu, wd, tokens, upstream = (
        pltpu.with_memory_space_constraint(a, pltpu.HBM) for a in (w_gate[0], w_up[0], w_down[0], tokens, upstream)
    )
    v = {}

    def sync(*names):
        v.update(zip(names, lax.optimization_barrier(tuple(v[n] for n in names))))

    def across(k, source, result):
        with jax.named_scope(f"{result}_{k}"):
            v[f"{result}{k}"] = lax.ppermute(v[f"{source}{k}"], "expert", [(i, i ^ k) for i in range(count)])

    def swap(value, k):
        return lax.ppermute(value, "tensor", [(i, i ^ k) for i in range(n_tensor)])

    def take(*ks):
        for k in ks:
            across(k, "send", "in")

    def forward(*ks):
        for k in ks:
            with jax.named_scope(f"forward_{k}"):
                v[f"fw{k}"] = swap(v[f"in{k}"], 2)

    def weights():
        return (v["wgu"], v["wd"], v["wguo"], v["wdo"])

    def project_chunk(c):
        blocks = CHUNKS[c]
        v[f"mine{c}"], sent = project(
            [v[f"in{k}"] for k in blocks], [v[f"fw{k}"] for k in blocks], weights()
        )
        v[f"other{c}"] = swap(sent, 1)

    def partner_chunk(c):
        blocks = CHUNKS[c]
        *pay, v[f"h{c}"] = partner_part(v[f"mine{c}"], v[f"other{c}"], weights(), width, len(blocks))
        v.update({f"part{k}": p for k, p in zip(blocks, pay)})

    def own_chunk(c):
        blocks = CHUNKS[c]
        own = own_part(v[f"h{c}"], weights(), width, len(blocks))
        v.update({f"own{k}": p for k, p in zip(blocks, own)})

    def pay(*ks):
        for k in ks:
            with jax.named_scope(f"pay_{k}"):
                v[f"pay{k}"] = swap(v[f"part{k}"], 2)

    def give(*ks):
        for k in ks:
            v[f"sum{k}"] = merge(v[f"own{k}"], v[f"pay{k}"])
            if k:
                across(k, "sum", "out")
            else:
                v["out0"] = v["sum0"]

    *sends, cut_gu, cut_d = dispatch(
        info, expert_ids.T, gates.T, tokens, upstream, wg, wu, wd, count, cap
    )
    v.update({f"send{k}": s for k, s in enumerate(sends)})
    v["in0"] = v["send0"]
    take(4, 1)
    forward(0)
    v["wguo"], v["wdo"] = swap(cut_gu, 1), swap(cut_d, 1)
    v["wgu"], v["wd"], pick, gate = cut_own(
        info, expert_ids.T, gates.T, wg, wu, wd, width, count, cap
    )
    sync("in1", "fw0", "send2", "wgu", "wd")
    take(2)
    forward(1)
    sync("in4", "send5")
    take(5)
    forward(4)
    sync("fw1", "in2", "send3", "wguo", "wdo")
    forward(2)
    take(3)
    project_chunk("A")
    sync("in5", "send6", "fw4")
    take(6)
    forward(5)
    partner_chunk("A")
    sync("fw2", "part4")
    pay(4)
    sync("in6", "send7", "part4")
    take(7)
    own_chunk("A")
    sync("pay4", "in3")
    forward(3)
    sync("fw5", "in6")
    forward(6)
    project_chunk("B")
    give(4)
    partner_chunk("B")
    own_chunk("B")
    sync("fw3", "part5")
    pay(5)
    sync("fw6", "in7")
    forward(7)
    project_chunk("C")
    partner_chunk("C")
    own_chunk("C")
    sync("fw7", "part6")
    pay(6)
    project_chunk("D")
    partner_chunk("D")
    sync("pay5", "part1", "own5", "out4")
    give(5)
    pay(1)
    sync("pay6", "part7", "own6")
    give(6)
    pay(7)
    own_chunk("D")
    sync("pay1", "part3")
    give(1)
    pay(3)
    sync("pay7", "part2", "own7", "out5")
    give(7)
    pay(2)
    sync("pay3", "part0", "out1")
    give(3)
    pay(0)
    give(2, 0)
    mixed, grad_tokens, inner = combine(pick, gate, upstream, [v[f"out{k}"] for k in range(count)])
    others = [swap(inner, k) for k in range(1, n_tensor)]
    return (mixed, grad_tokens, sum(others, inner).T)


def solution(mesh):
    fast = mesh.shape["expert"] == 8 and mesh.shape["tensor"] == 4
    return jax.shard_map(
        body_fast if fast else body_general,
        mesh=mesh,
        in_specs=(
            P("expert", "tensor"),
            P("expert", "tensor"),
            P("expert", None),
            P("expert", None),
            P("expert", None, "tensor"),
            P("expert", None, "tensor"),
            P("expert", "tensor", None),
        ),
        out_specs=(P("expert", "tensor"), P("expert", "tensor"), P("expert", None)),
        check_vma=False,
    )
```

```python
import functools
import jax
import jax.numpy as jnp
from jax import lax
from jax.experimental import pallas as pl
from jax.experimental.pallas import tpu as pltpu
from jax.sharding import PartitionSpec as P

F32 = jnp.float32
BF16 = jnp.bfloat16
VMEM_LIMIT = 20 << 20
COST = pl.CostEstimate(flops=1024, bytes_accessed=1024, transcendentals=0)


def contract_last(left, right):
    return lax.dot_general(left, right, (((1,), (1,)), ((), ())), preferred_element_type=F32)


def dot(left, right):
    return jnp.dot(left, right, preferred_element_type=F32)


def expert_work(row_x, row_dy, weight_gate, weight_up, weight_down):
    gate_pre = dot(row_x, weight_gate)
    up_pre = dot(row_x, weight_up)
    sigma = jax.nn.sigmoid(gate_pre)
    active = gate_pre * sigma
    hidden = (active * up_pre).astype(BF16)
    out_part = dot(hidden, weight_down).astype(BF16)
    grad_hidden = contract_last(row_dy, weight_down)
    grad_up = (grad_hidden * active).astype(BF16)
    grad_gate = (grad_hidden * up_pre * sigma * (1.0 + gate_pre * (1.0 - sigma))).astype(BF16)
    in_part = (contract_last(grad_gate, weight_gate) + contract_last(grad_up, weight_up)).astype(BF16)
    return (out_part, in_part)


def body_general(tokens, upstream, gates, expert_ids, w_gate, w_up, w_down):
    tok_dev = tokens.shape[0]
    expert_count = lax.axis_size("expert")
    capacity = max(2, 3 * tok_dev // expert_count)
    slot_count = expert_count * capacity
    entry_count = 2 * tok_dev
    flat_ids = expert_ids.reshape(entry_count)
    onehot = (flat_ids[:, None] == jnp.arange(expert_count, dtype=jnp.int32)[None, :]).astype(jnp.int32)
    before = jnp.cumsum(onehot, axis=0) - onehot
    position = jnp.sum(before * onehot, axis=1)
    slot_of_entry = flat_ids * capacity + position
    match = slot_of_entry[None, :] == jnp.arange(slot_count, dtype=jnp.int32)[:, None]
    entry_index = jnp.arange(entry_count, dtype=jnp.int32)
    entry_of_slot = jnp.sum(jnp.where(match, entry_index[None, :], 0), axis=1)
    slot_used = jnp.any(match, axis=1)[:, None]
    gate_flat = gates.reshape(entry_count)
    token_rows = entry_of_slot // 2
    send_x = jnp.where(slot_used, jnp.take(tokens, token_rows, axis=0), jnp.zeros((), BF16))
    scaled = (
        jnp.take(upstream, token_rows, axis=0).astype(F32) * jnp.take(gate_flat, entry_of_slot)[:, None]
    ).astype(BF16)
    send_dy = jnp.where(slot_used, scaled, jnp.zeros((), BF16))

    def exchange(value):
        return lax.all_to_all(value, "expert", split_axis=0, concat_axis=0, tiled=True)

    recv_x = lax.all_gather(exchange(send_x), "tensor", axis=1, tiled=True)
    recv_dy = lax.all_gather(exchange(send_dy), "tensor", axis=1, tiled=True)
    out_part, in_part = expert_work(recv_x, recv_dy, w_gate[0], w_up[0], w_down[0])
    back_out = exchange(lax.psum_scatter(out_part, "tensor", scatter_dimension=1, tiled=True))
    back_grad = exchange(lax.psum_scatter(in_part, "tensor", scatter_dimension=1, tiled=True))
    width = back_out.shape[1]
    entry_out = jnp.take(back_out, slot_of_entry, axis=0).reshape(tok_dev, 2, width).astype(F32)
    entry_grad = jnp.take(back_grad, slot_of_entry, axis=0).reshape(tok_dev, 2, width).astype(F32)
    mixed = (gates[:, 0:1] * entry_out[:, 0] + gates[:, 1:2] * entry_out[:, 1]).astype(BF16)
    grad_tokens = (entry_grad[:, 0] + entry_grad[:, 1]).astype(BF16)
    local_inner = jnp.sum(upstream.astype(F32)[:, None, :] * entry_out, axis=-1)
    return (mixed, grad_tokens, lax.psum(local_inner, "tensor"))


def cuts(t, flips, wg, wu, wd, gu, d, sems):
    width = d.shape[1] // 2
    for j, flip in enumerate(flips):
        start = pl.multiple_of(jnp.bitwise_xor(t, flip) * width, width)
        to = pl.ds(j * width, width)
        yield pltpu.make_async_copy(wg.at[pl.ds(start, width)], gu.at[0, to], sems.at[3 * j])
        yield pltpu.make_async_copy(wu.at[pl.ds(start, width)], gu.at[1, to], sems.at[3 * j + 1])
        yield pltpu.make_async_copy(wd.at[:, pl.ds(start, width)], d.at[:, to], sems.at[3 * j + 2])


def cut_kernel(info, ids_ref, gates_ref, wg, wu, wd, gu, d, pick, gate, sems, *, count):
    copies = list(cuts(info[1], (0, 2), wg, wu, wd, gu, d, sems))
    for copy in copies:
        copy.start()
    tok_dev, slots = pick.shape[1:]
    near = jnp.bitwise_xor(ids_ref[...], info[0]).astype(F32)
    columns = jnp.transpose(jnp.concatenate([near, gates_ref[...], jnp.zeros((4, tok_dev), F32)], axis=0))
    gate[...] = columns
    first, second = columns[:, 0:1].astype(jnp.int32), columns[:, 1:2].astype(jnp.int32)
    which = lax.broadcasted_iota(jnp.int32, (tok_dev, count), 1)
    named = jnp.where((which == first) | (which == second), 1.0, 0.0)
    earlier = lax.broadcasted_iota(jnp.int32, (tok_dev, tok_dev), 1) < lax.broadcasted_iota(
        jnp.int32, (tok_dev, tok_dev), 0
    )
    before = dot(jnp.where(earlier, 1.0, 0.0).astype(BF16), named.astype(BF16))
    lane = lax.broadcasted_iota(jnp.int32, (tok_dev, slots), 1).astype(F32)
    for j, near_k in enumerate((first, second)):
        place = jnp.sum(jnp.where(which == near_k, before, 0.0), axis=1, keepdims=True)
        pick[j] = jnp.where(lane == near_k.astype(F32) * (slots // count) + place, 1.0, 0.0).astype(BF16)
    for copy in copies:
        copy.wait()


def cut_shapes(wg, width):
    hw = wg.shape[1]
    return [jax.ShapeDtypeStruct((2, 2 * width, hw), BF16), jax.ShapeDtypeStruct((hw, 2 * width), BF16)]


def cut_own(info, ids_t, gates_t, wg, wu, wd, width, count, cap):
    tok_dev = ids_t.shape[1]
    vmem = pl.BlockSpec(memory_space=pltpu.VMEM)
    return pl.pallas_call(
        functools.partial(cut_kernel, count=count),
        out_shape=cut_shapes(wg, width)
        + [
            jax.ShapeDtypeStruct((2, tok_dev, count * cap), BF16),
            jax.ShapeDtypeStruct((tok_dev, 8), F32),
        ],
        in_specs=[pl.BlockSpec(memory_space=pltpu.SMEM), vmem, vmem]
        + [pl.BlockSpec(memory_space=pl.ANY)] * 3,
        out_specs=[vmem] * 4,
        scratch_shapes=[pltpu.SemaphoreType.DMA((6,))],
        compiler_params=pltpu.CompilerParams(vmem_limit_bytes=VMEM_LIMIT),
        cost_estimate=pl.CostEstimate(flops=0, bytes_accessed=24 * width * wg.shape[1], transcendentals=0),
        name="cut_own",
    )(info, ids_t, gates_t, wg, wu, wd)


def dispatch_kernel(info, ids_hbm, gates_hbm, tok_hbm, up_hbm, wg, wu, wd, *refs, count, cap):
    outs, cut_gu, cut_d, ids_ref, gates_ref, tok, up, sel, gsl, sems = refs[:count], *refs[count:]
    tok_dev = ids_ref.shape[1]
    small = [
        pltpu.make_async_copy(ids_hbm, ids_ref, sems.at[8]),
        pltpu.make_async_copy(gates_hbm, gates_ref, sems.at[9]),
    ]
    loads = [
        pltpu.make_async_copy(tok_hbm, tok, sems.at[6]),
        pltpu.make_async_copy(up_hbm, up, sems.at[7]),
    ]
    copies = list(cuts(info[1], (1, 3), wg, wu, wd, cut_gu, cut_d, sems))
    for copy in small + loads + copies:
        copy.start()

    for copy in small:
        copy.wait()
    near = jnp.bitwise_xor(ids_ref[...], info[0])
    first, second = near[0:1, :], near[1:2, :]
    which = lax.broadcasted_iota(jnp.int32, (count, tok_dev), 0)
    named = jnp.where((which == first) | (which == second), 1.0, 0.0)
    earlier = lax.broadcasted_iota(jnp.int32, (tok_dev, tok_dev), 0) < lax.broadcasted_iota(
        jnp.int32, (tok_dev, tok_dev), 1
    )
    before = dot(named.astype(BF16), jnp.where(earlier, 1.0, 0.0).astype(BF16))
    gate = jnp.where(which == first, gates_ref[0:1, :], gates_ref[1:2, :])
    slot = lax.broadcasted_iota(jnp.int32, (cap, tok_dev), 0).astype(F32)
    for k in range(count):
        hit = (before[k : k + 1, :] == slot) & (named[k : k + 1, :] > 0.5)
        sel[k * cap : (k + 1) * cap, :] = jnp.where(hit, 1.0, 0.0).astype(BF16)
        gsl[k * cap : (k + 1) * cap, :] = jnp.sum(
            jnp.where(hit, jnp.broadcast_to(gate[k : k + 1, :], hit.shape), 0.0), axis=1, keepdims=True
        )

    loads[0].wait()
    for k in range(count):
        outs[k][0] = dot(sel[k * cap : (k + 1) * cap], tok[...]).astype(BF16)
    loads[1].wait()
    for k in range(count):
        rows = slice(k * cap, (k + 1) * cap)
        outs[k][1] = (dot(sel[rows], up[...]) * gsl[rows]).astype(BF16)
    for copy in copies:
        copy.wait()


def dispatch(info, ids_t, gates_t, tokens, upstream, wg, wu, wd, count, cap):
    tok_dev, width = tokens.shape
    outs = [jax.ShapeDtypeStruct((2, cap, width), BF16)] * count + cut_shapes(wg, width)
    return pl.pallas_call(
        functools.partial(dispatch_kernel, count=count, cap=cap),
        out_shape=outs,
        in_specs=[pl.BlockSpec(memory_space=pltpu.SMEM)]
        + [pl.BlockSpec(memory_space=pl.ANY)] * 7,
        out_specs=[pl.BlockSpec(memory_space=pltpu.VMEM)] * len(outs),
        scratch_shapes=[
            pltpu.VMEM((2, tok_dev), jnp.int32),
            pltpu.VMEM((2, tok_dev), F32),
            pltpu.VMEM((tok_dev, width), BF16),
            pltpu.VMEM((tok_dev, width), BF16),
            pltpu.VMEM((count * cap, tok_dev), BF16),
            pltpu.VMEM((count * cap, 1), F32),
            pltpu.SemaphoreType.DMA((10,)),
        ],
        compiler_params=pltpu.CompilerParams(vmem_limit_bytes=VMEM_LIMIT),
        cost_estimate=COST,
        name="dispatch",
    )(info, ids_t, gates_t, tokens, upstream, wg, wu, wd)


def project_kernel(*refs, m):
    own, fwd = refs[:m], refs[m : 2 * m]
    own_gu, own_d, far_gu, far_d, out, sent = refs[2 * m :]
    cap, width = own[0].shape[1:]
    hw = own_d.shape[0]
    x = [jnp.concatenate([b[0] for b in blocks], axis=0) for blocks in (own, fwd)]
    dy = [jnp.concatenate([b[1] for b in blocks], axis=0) for blocks in (own, fwd)]
    for j, (gu, d) in enumerate(((own_gu, own_d), (far_gu, far_d))):
        for p, part in enumerate(
            (
                dot(x[0], gu[0, :width]) + dot(x[1], gu[0, width:]),
                dot(x[0], gu[1, :width]) + dot(x[1], gu[1, width:]),
                contract_last(dy[0], d[:, :width]) + contract_last(dy[1], d[:, width:]),
            )
        ):
            cols = slice((2 * p + j) * hw, (2 * p + j + 1) * hw)
            out[:, cols] = part
            sent[:, cols] = part.astype(BF16)


def whole(kernel, outs, name, *args):
    return pl.pallas_call(
        kernel,
        out_shape=outs,
        in_specs=[pl.BlockSpec(memory_space=pltpu.VMEM)] * len(args),
        out_specs=[pl.BlockSpec(memory_space=pltpu.VMEM)] * len(outs),
        compiler_params=pltpu.CompilerParams(vmem_limit_bytes=VMEM_LIMIT),
        cost_estimate=COST,
        name=name,
    )(*args)


def project(own, fwd, weights):
    m = len(own)
    rows, six = m * own[0].shape[1], 6 * weights[1].shape[0]
    outs = [jax.ShapeDtypeStruct((rows, six), F32), jax.ShapeDtypeStruct((rows, six), BF16)]
    return whole(functools.partial(project_kernel, m=m), outs, "project", *own, *fwd, *weights)


def emit(h3, own_gu, own_d, far_gu, far_d, pays, side):
    hw = own_d.shape[0]
    cap, width = pays[0].shape[1:]
    cols = slice(side * width, (side + 1) * width)
    out = dot(h3[0, :, :hw], own_d[:, cols]) + dot(h3[0, :, hw:], far_d[:, cols])
    for j, pay in enumerate(pays):
        pay[0] = out[j * cap : (j + 1) * cap].astype(BF16)
    grad = (
        contract_last(h3[1, :, :hw], own_gu[0, cols])
        + contract_last(h3[1, :, hw:], far_gu[0, cols])
        + contract_last(h3[2, :, :hw], own_gu[1, cols])
        + contract_last(h3[2, :, hw:], far_gu[1, cols])
    )
    for j, pay in enumerate(pays):
        pay[1] = grad[j * cap : (j + 1) * cap].astype(BF16)


def partner_kernel(mine, other, own_gu, own_d, far_gu, far_d, *outs):
    pays, h3 = outs[:-1], outs[-1]
    hw = own_d.shape[0]
    for b in range(2):
        def total(j):
            lo, sw = (2 * j + b) * hw, (2 * j + 1 - b) * hw
            return mine[:, lo : lo + hw] + other[:, sw : sw + hw].astype(F32)

        gate_pre, up_pre, grad_hidden = total(0), total(1), total(2)
        sigma = jax.nn.sigmoid(gate_pre)
        active = gate_pre * sigma
        cols = slice(b * hw, (b + 1) * hw)
        h3[0, :, cols] = (active * up_pre).astype(BF16)
        h3[1, :, cols] = (grad_hidden * up_pre * sigma * (1.0 + gate_pre * (1.0 - sigma))).astype(BF16)
        h3[2, :, cols] = (grad_hidden * active).astype(BF16)
    emit(h3, own_gu, own_d, far_gu, far_d, pays, 1)


def own_kernel(h3, own_gu, own_d, far_gu, far_d, *pays):
    emit(h3, own_gu, own_d, far_gu, far_d, pays, 0)


def partner_part(mine, other, weights, width, m):
    rows, six = mine.shape
    outs = [jax.ShapeDtypeStruct((2, rows // m, width), BF16)] * m
    outs.append(jax.ShapeDtypeStruct((3, rows, six // 3), BF16))
    return whole(partner_kernel, outs, "partner_part", mine, other, *weights)


def own_part(h3, weights, width, m):
    rows = h3.shape[1]
    outs = [jax.ShapeDtypeStruct((2, rows // m, width), BF16)] * m
    return whole(own_kernel, outs, "own_part", h3, *weights)


def merge(a, b):
    return (a.astype(F32) + b.astype(F32)).astype(BF16)


def mixed_kernel(pick, gate, up, *refs):
    blocks, mixed_hbm, inner, mixed, sems = refs[:-4], *refs[-4:]
    tok_dev, width = mixed.shape
    parts = 2
    blk = width // parts
    copies, sums = [], [0.0, 0.0]
    for p in range(parts):
        cols = slice(p * blk, (p + 1) * blk)
        outs = jnp.concatenate([b[0, :, cols] for b in blocks], axis=0)
        entries = [dot(pick[j], outs) for j in range(2)]
        mixed[:, cols] = (gate[:, 2:3] * entries[0] + gate[:, 3:4] * entries[1]).astype(BF16)
        copies.append(pltpu.make_async_copy(mixed.at[:, cols], mixed_hbm.at[:, cols], sems.at[p]))
        copies[-1].start()
        cotangent = up[:, cols].astype(F32)
        for j in range(2):
            sums[j] = sums[j] + jnp.sum(cotangent * entries[j], axis=1, keepdims=True)
    spot = lax.broadcasted_iota(jnp.int32, (tok_dev, 128), 1)
    side = jnp.where(spot == 0, sums[0], jnp.where(spot == 1, sums[1], 0.0))
    inner[...] = jnp.transpose(side)[:2, :]
    for copy in copies:
        copy.wait()


def grad_kernel(pick, *refs):
    blocks, grad_hbm, grad, sems = refs[:-3], *refs[-3:]
    width = grad.shape[1]
    parts = 2
    blk = width // parts
    both = pick[0] + pick[1]
    copies = []
    for p in range(parts):
        cols = slice(p * blk, (p + 1) * blk)
        grads = jnp.concatenate([b[1, :, cols] for b in blocks], axis=0)
        grad[:, cols] = dot(both, grads).astype(BF16)
        copies.append(pltpu.make_async_copy(grad.at[:, cols], grad_hbm.at[:, cols], sems.at[p]))
        copies[-1].start()
    for copy in copies:
        copy.wait()


def combine(pick, gate, upstream, blocks):
    tok_dev = pick.shape[1]
    width = blocks[0].shape[2]
    vmem, anywhere = pl.BlockSpec(memory_space=pltpu.VMEM), pl.BlockSpec(memory_space=pl.ANY)
    full = jax.ShapeDtypeStruct((tok_dev, width), BF16)
    scratch = [pltpu.VMEM((tok_dev, width), BF16), pltpu.SemaphoreType.DMA((2,))]
    params = pltpu.CompilerParams(vmem_limit_bytes=VMEM_LIMIT)
    mixed, inner = pl.pallas_call(
        mixed_kernel,
        out_shape=[full, jax.ShapeDtypeStruct((2, tok_dev), F32)],
        in_specs=[vmem] * (3 + len(blocks)),
        out_specs=[anywhere, vmem],
        scratch_shapes=scratch,
        compiler_params=params,
        cost_estimate=COST,
        name="mixed",
    )(pick, gate, upstream, *blocks)
    grad = pl.pallas_call(
        grad_kernel,
        out_shape=full,
        in_specs=[vmem] * (1 + len(blocks)),
        out_specs=anywhere,
        scratch_shapes=scratch,
        compiler_params=params,
        cost_estimate=pl.CostEstimate(flops=0, bytes_accessed=16 << 20, transcendentals=0),
        name="grad",
    )(pick, *blocks)
    return mixed, grad, inner


CHUNKS = {"A": (0, 1, 4), "B": (2, 5), "C": (3, 6), "D": (7,)}


def body_fast(tokens, upstream, gates, expert_ids, w_gate, w_up, w_down):
    count, n_tensor = lax.axis_size("expert"), lax.axis_size("tensor")
    tok_dev, width = tokens.shape
    cap = 3 * tok_dev // count
    me, t = lax.axis_index("expert"), lax.axis_index("tensor")
    info = jnp.stack([me, t]).astype(jnp.int32)
    wg, wu, wd, tokens, upstream, ids_t, gates_t = (
        pltpu.with_memory_space_constraint(a, pltpu.HBM)
        for a in (w_gate[0], w_up[0], w_down[0], tokens, upstream, expert_ids.T, gates.T)
    )
    v = {}

    def sync(*names):
        v.update(zip(names, lax.optimization_barrier(tuple(v[n] for n in names))))

    def across(k, source, result):
        with jax.named_scope(f"{result}_{k}"):
            v[f"{result}{k}"] = lax.ppermute(v[f"{source}{k}"], "expert", [(i, i ^ k) for i in range(count)])

    def swap(value, k):
        return lax.ppermute(value, "tensor", [(i, i ^ k) for i in range(n_tensor)])

    def take(*ks):
        for k in ks:
            across(k, "send", "in")

    def forward(*ks):
        for k in ks:
            with jax.named_scope(f"forward_{k}"):
                v[f"fw{k}"] = swap(v[f"in{k}"], 2)

    def weights():
        return (v["wgu"], v["wd"], v["wguo"], v["wdo"])

    def project_chunk(c):
        blocks = CHUNKS[c]
        v[f"mine{c}"], sent = project(
            [v[f"in{k}"] for k in blocks], [v[f"fw{k}"] for k in blocks], weights()
        )
        v[f"other{c}"] = swap(sent, 1)

    def partner_chunk(c):
        blocks = CHUNKS[c]
        *pay, v[f"h{c}"] = partner_part(v[f"mine{c}"], v[f"other{c}"], weights(), width, len(blocks))
        v.update({f"part{k}": p for k, p in zip(blocks, pay)})

    def own_chunk(c):
        blocks = CHUNKS[c]
        own = own_part(v[f"h{c}"], weights(), width, len(blocks))
        v.update({f"own{k}": p for k, p in zip(blocks, own)})

    def pay(*ks):
        for k in ks:
            with jax.named_scope(f"pay_{k}"):
                v[f"pay{k}"] = swap(v[f"part{k}"], 2)

    def give(*ks):
        for k in ks:
            v[f"sum{k}"] = merge(v[f"own{k}"], v[f"pay{k}"])
            if k:
                across(k, "sum", "out")
            else:
                v["out0"] = v["sum0"]

    *sends, cut_gu, cut_d = dispatch(
        info, ids_t, gates_t, tokens, upstream, wg, wu, wd, count, cap
    )
    v.update({f"send{k}": s for k, s in enumerate(sends)})
    v["in0"] = v["send0"]
    take(4, 1)
    forward(0)
    v["wguo"], v["wdo"] = swap(cut_gu, 1), swap(cut_d, 1)
    v["wgu"], v["wd"], pick, gate = cut_own(
        info, expert_ids.T, gates.T, wg, wu, wd, width, count, cap
    )
    sync("in1", "fw0", "send2", "wgu", "wd")
    take(2)
    forward(1)
    sync("in4", "send5")
    take(5)
    forward(4)
    sync("fw1", "in2", "send3", "wguo", "wdo")
    forward(2)
    take(3)
    project_chunk("A")
    sync("in5", "send6", "fw4")
    take(6)
    forward(5)
    partner_chunk("A")
    sync("fw2", "part4")
    pay(4)
    sync("in6", "send7", "part4")
    take(7)
    own_chunk("A")
    sync("pay4", "in3")
    forward(3)
    sync("fw5", "in6")
    forward(6)
    project_chunk("B")
    give(4)
    partner_chunk("B")
    own_chunk("B")
    sync("fw3", "part5")
    pay(5)
    sync("fw6", "in7")
    forward(7)
    project_chunk("C")
    partner_chunk("C")
    own_chunk("C")
    sync("fw7", "part6")
    pay(6)
    project_chunk("D")
    partner_chunk("D")
    sync("pay5", "part1", "own5", "out4")
    give(5)
    pay(1)
    sync("pay6", "part7", "own6")
    give(6)
    pay(7)
    own_chunk("D")
    sync("pay1", "part2")
    give(1)
    pay(2)
    sync("pay7", "part3", "own7")
    give(7)
    pay(3)
    sync("pay2", "part0", "out1", "out5")
    give(2)
    pay(0)
    give(3, 0)
    mixed, grad_tokens, inner = combine(pick, gate, upstream, [v[f"out{k}"] for k in range(count)])
    others = [swap(inner, k) for k in range(1, n_tensor)]
    return (mixed, grad_tokens, sum(others, inner).T)


def solution(mesh):
    fast = mesh.shape["expert"] == 8 and mesh.shape["tensor"] == 4
    return jax.shard_map(
        body_fast if fast else body_general,
        mesh=mesh,
        in_specs=(
            P("expert", "tensor"),
            P("expert", "tensor"),
            P("expert", None),
            P("expert", None),
            P("expert", None, "tensor"),
            P("expert", None, "tensor"),
            P("expert", "tensor", None),
        ),
        out_specs=(P("expert", "tensor"), P("expert", "tensor"), P("expert", None)),
        check_vma=False,
    )
```

```python
import functools
import jax
import jax.numpy as jnp
from jax import lax
from jax.experimental import pallas as pl
from jax.experimental.pallas import tpu as pltpu
from jax.sharding import PartitionSpec as P

F32 = jnp.float32
BF16 = jnp.bfloat16
VMEM_LIMIT = 20 << 20
COST = pl.CostEstimate(flops=1024, bytes_accessed=1024, transcendentals=0)


def contract_last(left, right):
    return lax.dot_general(left, right, (((1,), (1,)), ((), ())), preferred_element_type=F32)


def dot(left, right):
    return jnp.dot(left, right, preferred_element_type=F32)


def expert_work(row_x, row_dy, weight_gate, weight_up, weight_down):
    gate_pre = dot(row_x, weight_gate)
    up_pre = dot(row_x, weight_up)
    sigma = jax.nn.sigmoid(gate_pre)
    active = gate_pre * sigma
    hidden = (active * up_pre).astype(BF16)
    out_part = dot(hidden, weight_down).astype(BF16)
    grad_hidden = contract_last(row_dy, weight_down)
    grad_up = (grad_hidden * active).astype(BF16)
    grad_gate = (grad_hidden * up_pre * sigma * (1.0 + gate_pre * (1.0 - sigma))).astype(BF16)
    in_part = (contract_last(grad_gate, weight_gate) + contract_last(grad_up, weight_up)).astype(BF16)
    return (out_part, in_part)


def body_general(tokens, upstream, gates, expert_ids, w_gate, w_up, w_down):
    tok_dev = tokens.shape[0]
    expert_count = lax.axis_size("expert")
    capacity = max(2, 3 * tok_dev // expert_count)
    slot_count = expert_count * capacity
    entry_count = 2 * tok_dev
    flat_ids = expert_ids.reshape(entry_count)
    onehot = (flat_ids[:, None] == jnp.arange(expert_count, dtype=jnp.int32)[None, :]).astype(jnp.int32)
    before = jnp.cumsum(onehot, axis=0) - onehot
    position = jnp.sum(before * onehot, axis=1)
    slot_of_entry = flat_ids * capacity + position
    match = slot_of_entry[None, :] == jnp.arange(slot_count, dtype=jnp.int32)[:, None]
    entry_index = jnp.arange(entry_count, dtype=jnp.int32)
    entry_of_slot = jnp.sum(jnp.where(match, entry_index[None, :], 0), axis=1)
    slot_used = jnp.any(match, axis=1)[:, None]
    gate_flat = gates.reshape(entry_count)
    token_rows = entry_of_slot // 2
    send_x = jnp.where(slot_used, jnp.take(tokens, token_rows, axis=0), jnp.zeros((), BF16))
    scaled = (
        jnp.take(upstream, token_rows, axis=0).astype(F32) * jnp.take(gate_flat, entry_of_slot)[:, None]
    ).astype(BF16)
    send_dy = jnp.where(slot_used, scaled, jnp.zeros((), BF16))

    def exchange(value):
        return lax.all_to_all(value, "expert", split_axis=0, concat_axis=0, tiled=True)

    recv_x = lax.all_gather(exchange(send_x), "tensor", axis=1, tiled=True)
    recv_dy = lax.all_gather(exchange(send_dy), "tensor", axis=1, tiled=True)
    out_part, in_part = expert_work(recv_x, recv_dy, w_gate[0], w_up[0], w_down[0])
    back_out = exchange(lax.psum_scatter(out_part, "tensor", scatter_dimension=1, tiled=True))
    back_grad = exchange(lax.psum_scatter(in_part, "tensor", scatter_dimension=1, tiled=True))
    width = back_out.shape[1]
    entry_out = jnp.take(back_out, slot_of_entry, axis=0).reshape(tok_dev, 2, width).astype(F32)
    entry_grad = jnp.take(back_grad, slot_of_entry, axis=0).reshape(tok_dev, 2, width).astype(F32)
    mixed = (gates[:, 0:1] * entry_out[:, 0] + gates[:, 1:2] * entry_out[:, 1]).astype(BF16)
    grad_tokens = (entry_grad[:, 0] + entry_grad[:, 1]).astype(BF16)
    local_inner = jnp.sum(upstream.astype(F32)[:, None, :] * entry_out, axis=-1)
    return (mixed, grad_tokens, lax.psum(local_inner, "tensor"))


def cuts(t, flips, wg, wu, wd, gu, d, sems):
    width = d.shape[1] // 2
    for j, flip in enumerate(flips):
        start = pl.multiple_of(jnp.bitwise_xor(t, flip) * width, width)
        to = pl.ds(j * width, width)
        yield pltpu.make_async_copy(wg.at[pl.ds(start, width)], gu.at[0, to], sems.at[3 * j])
        yield pltpu.make_async_copy(wu.at[pl.ds(start, width)], gu.at[1, to], sems.at[3 * j + 1])
        yield pltpu.make_async_copy(wd.at[:, pl.ds(start, width)], d.at[:, to], sems.at[3 * j + 2])


def cut_kernel(info, ids_ref, gates_ref, wg, wu, wd, gu, d, pick, gate, sems, *, count):
    copies = list(cuts(info[1], (0, 2), wg, wu, wd, gu, d, sems))
    for copy in copies:
        copy.start()
    tok_dev, slots = pick.shape[1:]
    near = jnp.bitwise_xor(ids_ref[...], info[0]).astype(F32)
    columns = jnp.transpose(jnp.concatenate([near, gates_ref[...], jnp.zeros((4, tok_dev), F32)], axis=0))
    gate[...] = columns
    first, second = columns[:, 0:1].astype(jnp.int32), columns[:, 1:2].astype(jnp.int32)
    which = lax.broadcasted_iota(jnp.int32, (tok_dev, count), 1)
    named = jnp.where((which == first) | (which == second), 1.0, 0.0)
    earlier = lax.broadcasted_iota(jnp.int32, (tok_dev, tok_dev), 1) < lax.broadcasted_iota(
        jnp.int32, (tok_dev, tok_dev), 0
    )
    before = dot(jnp.where(earlier, 1.0, 0.0).astype(BF16), named.astype(BF16))
    lane = lax.broadcasted_iota(jnp.int32, (tok_dev, slots), 1).astype(F32)
    for j, near_k in enumerate((first, second)):
        place = jnp.sum(jnp.where(which == near_k, before, 0.0), axis=1, keepdims=True)
        pick[j] = jnp.where(lane == near_k.astype(F32) * (slots // count) + place, 1.0, 0.0).astype(BF16)
    for copy in copies:
        copy.wait()


def cut_shapes(wg, width):
    hw = wg.shape[1]
    return [jax.ShapeDtypeStruct((2, 2 * width, hw), BF16), jax.ShapeDtypeStruct((hw, 2 * width), BF16)]


def cut_own(info, ids_t, gates_t, wg, wu, wd, width, count, cap):
    tok_dev = ids_t.shape[1]
    vmem = pl.BlockSpec(memory_space=pltpu.VMEM)
    return pl.pallas_call(
        functools.partial(cut_kernel, count=count),
        out_shape=cut_shapes(wg, width)
        + [
            jax.ShapeDtypeStruct((2, tok_dev, count * cap), BF16),
            jax.ShapeDtypeStruct((tok_dev, 8), F32),
        ],
        in_specs=[pl.BlockSpec(memory_space=pltpu.SMEM), vmem, vmem]
        + [pl.BlockSpec(memory_space=pl.ANY)] * 3,
        out_specs=[vmem] * 4,
        scratch_shapes=[pltpu.SemaphoreType.DMA((6,))],
        compiler_params=pltpu.CompilerParams(vmem_limit_bytes=VMEM_LIMIT),
        cost_estimate=pl.CostEstimate(flops=0, bytes_accessed=24 * width * wg.shape[1], transcendentals=0),
        name="cut_own",
    )(info, ids_t, gates_t, wg, wu, wd)


def dispatch_kernel(info, ids_hbm, gates_hbm, tok_hbm, up_hbm, wg, wu, wd, *refs, count, cap):
    outs, cut_gu, cut_d, ids_ref, gates_ref, tok, up, sel, gsl, sems = refs[:count], *refs[count:]
    tok_dev = ids_ref.shape[1]
    small = [
        pltpu.make_async_copy(ids_hbm, ids_ref, sems.at[8]),
        pltpu.make_async_copy(gates_hbm, gates_ref, sems.at[9]),
    ]
    loads = [
        pltpu.make_async_copy(tok_hbm, tok, sems.at[6]),
        pltpu.make_async_copy(up_hbm, up, sems.at[7]),
    ]
    copies = list(cuts(info[1], (1, 3), wg, wu, wd, cut_gu, cut_d, sems))
    for copy in small + loads + copies:
        copy.start()

    for copy in small:
        copy.wait()
    near = jnp.bitwise_xor(ids_ref[...], info[0])
    first, second = near[0:1, :], near[1:2, :]
    which = lax.broadcasted_iota(jnp.int32, (count, tok_dev), 0)
    named = jnp.where((which == first) | (which == second), 1.0, 0.0)
    earlier = lax.broadcasted_iota(jnp.int32, (tok_dev, tok_dev), 0) < lax.broadcasted_iota(
        jnp.int32, (tok_dev, tok_dev), 1
    )
    before = dot(named.astype(BF16), jnp.where(earlier, 1.0, 0.0).astype(BF16))
    gate = jnp.where(which == first, gates_ref[0:1, :], gates_ref[1:2, :])
    slot = lax.broadcasted_iota(jnp.int32, (cap, tok_dev), 0).astype(F32)
    for k in range(count):
        hit = (before[k : k + 1, :] == slot) & (named[k : k + 1, :] > 0.5)
        sel[k * cap : (k + 1) * cap, :] = jnp.where(hit, 1.0, 0.0).astype(BF16)
        gsl[k * cap : (k + 1) * cap, :] = jnp.sum(
            jnp.where(hit, jnp.broadcast_to(gate[k : k + 1, :], hit.shape), 0.0), axis=1, keepdims=True
        )

    loads[0].wait()
    for k in range(count):
        outs[k][0] = dot(sel[k * cap : (k + 1) * cap], tok[...]).astype(BF16)
    loads[1].wait()
    for k in range(count):
        rows = slice(k * cap, (k + 1) * cap)
        outs[k][1] = (dot(sel[rows], up[...]) * gsl[rows]).astype(BF16)
    for copy in copies:
        copy.wait()


def dispatch(info, ids_t, gates_t, tokens, upstream, wg, wu, wd, count, cap):
    tok_dev, width = tokens.shape
    outs = [jax.ShapeDtypeStruct((2, cap, width), BF16)] * count + cut_shapes(wg, width)
    return pl.pallas_call(
        functools.partial(dispatch_kernel, count=count, cap=cap),
        out_shape=outs,
        in_specs=[pl.BlockSpec(memory_space=pltpu.SMEM)]
        + [pl.BlockSpec(memory_space=pl.ANY)] * 7,
        out_specs=[pl.BlockSpec(memory_space=pltpu.VMEM)] * len(outs),
        scratch_shapes=[
            pltpu.VMEM((2, tok_dev), jnp.int32),
            pltpu.VMEM((2, tok_dev), F32),
            pltpu.VMEM((tok_dev, width), BF16),
            pltpu.VMEM((tok_dev, width), BF16),
            pltpu.VMEM((count * cap, tok_dev), BF16),
            pltpu.VMEM((count * cap, 1), F32),
            pltpu.SemaphoreType.DMA((10,)),
        ],
        compiler_params=pltpu.CompilerParams(vmem_limit_bytes=VMEM_LIMIT),
        cost_estimate=COST,
        name="dispatch",
    )(info, ids_t, gates_t, tokens, upstream, wg, wu, wd)


def project_kernel(*refs, m):
    own, fwd = refs[:m], refs[m : 2 * m]
    own_gu, own_d, far_gu, far_d, out, sent = refs[2 * m :]
    cap, width = own[0].shape[1:]
    hw = own_d.shape[0]
    x = [jnp.concatenate([b[0] for b in blocks], axis=0) for blocks in (own, fwd)]
    dy = [jnp.concatenate([b[1] for b in blocks], axis=0) for blocks in (own, fwd)]
    for j, (gu, d) in enumerate(((own_gu, own_d), (far_gu, far_d))):
        for p, part in enumerate(
            (
                dot(x[0], gu[0, :width]) + dot(x[1], gu[0, width:]),
                dot(x[0], gu[1, :width]) + dot(x[1], gu[1, width:]),
                contract_last(dy[0], d[:, :width]) + contract_last(dy[1], d[:, width:]),
            )
        ):
            cols = slice((2 * p + j) * hw, (2 * p + j + 1) * hw)
            out[:, cols] = part
            sent[:, cols] = part.astype(BF16)


def whole(kernel, outs, name, *args):
    return pl.pallas_call(
        kernel,
        out_shape=outs,
        in_specs=[pl.BlockSpec(memory_space=pltpu.VMEM)] * len(args),
        out_specs=[pl.BlockSpec(memory_space=pltpu.VMEM)] * len(outs),
        compiler_params=pltpu.CompilerParams(vmem_limit_bytes=VMEM_LIMIT),
        cost_estimate=COST,
        name=name,
    )(*args)


def project(own, fwd, weights):
    m = len(own)
    rows, six = m * own[0].shape[1], 6 * weights[1].shape[0]
    outs = [jax.ShapeDtypeStruct((rows, six), F32), jax.ShapeDtypeStruct((rows, six), BF16)]
    return whole(functools.partial(project_kernel, m=m), outs, "project", *own, *fwd, *weights)


def emit(h3, own_gu, own_d, far_gu, far_d, pays, side):
    hw = own_d.shape[0]
    cap, width = pays[0].shape[1:]
    cols = slice(side * width, (side + 1) * width)
    out = dot(h3[0, :, :hw], own_d[:, cols]) + dot(h3[0, :, hw:], far_d[:, cols])
    for j, pay in enumerate(pays):
        pay[0] = out[j * cap : (j + 1) * cap].astype(BF16)
    grad = (
        contract_last(h3[1, :, :hw], own_gu[0, cols])
        + contract_last(h3[1, :, hw:], far_gu[0, cols])
        + contract_last(h3[2, :, :hw], own_gu[1, cols])
        + contract_last(h3[2, :, hw:], far_gu[1, cols])
    )
    for j, pay in enumerate(pays):
        pay[1] = grad[j * cap : (j + 1) * cap].astype(BF16)


def partner_kernel(mine, other, own_gu, own_d, far_gu, far_d, *outs):
    pays, h3 = outs[:-1], outs[-1]
    hw = own_d.shape[0]
    for b in range(2):
        def total(j):
            lo, sw = (2 * j + b) * hw, (2 * j + 1 - b) * hw
            return mine[:, lo : lo + hw] + other[:, sw : sw + hw].astype(F32)

        gate_pre, up_pre, grad_hidden = total(0), total(1), total(2)
        sigma = jax.nn.sigmoid(gate_pre)
        active = gate_pre * sigma
        cols = slice(b * hw, (b + 1) * hw)
        h3[0, :, cols] = (active * up_pre).astype(BF16)
        h3[1, :, cols] = (grad_hidden * up_pre * sigma * (1.0 + gate_pre * (1.0 - sigma))).astype(BF16)
        h3[2, :, cols] = (grad_hidden * active).astype(BF16)
    emit(h3, own_gu, own_d, far_gu, far_d, pays, 1)


def own_kernel(h3, own_gu, own_d, far_gu, far_d, *pays):
    emit(h3, own_gu, own_d, far_gu, far_d, pays, 0)


def partner_part(mine, other, weights, width, m):
    rows, six = mine.shape
    outs = [jax.ShapeDtypeStruct((2, rows // m, width), BF16)] * m
    outs.append(jax.ShapeDtypeStruct((3, rows, six // 3), BF16))
    return whole(partner_kernel, outs, "partner_part", mine, other, *weights)


def own_part(h3, weights, width, m):
    rows = h3.shape[1]
    outs = [jax.ShapeDtypeStruct((2, rows // m, width), BF16)] * m
    return whole(own_kernel, outs, "own_part", h3, *weights)


def merge(a, b):
    return (a.astype(F32) + b.astype(F32)).astype(BF16)


def columns_of(pick, ks, cap):
    return jnp.concatenate([pick[:, k * cap : (k + 1) * cap] for k in ks], axis=1)


def early_kernel(pick, *refs, ks):
    blocks, entries, grad = refs[:-2], refs[-2], refs[-1]
    cap = blocks[0].shape[1]
    first, second = (columns_of(pick[j], ks, cap) for j in range(2))
    outs = jnp.concatenate([b[0] for b in blocks], axis=0)
    entries[0] = dot(first, outs)
    entries[1] = dot(second, outs)
    grad[...] = dot(first + second, jnp.concatenate([b[1] for b in blocks], axis=0))


def mixed_kernel(pick, gate, up, entries, *refs, ks):
    blocks, mixed, inner = refs[:-2], *refs[-2:]
    tok_dev = mixed.shape[0]
    cap = blocks[0].shape[1]
    outs = jnp.concatenate([b[0] for b in blocks], axis=0)
    entry = [entries[j] + dot(columns_of(pick[j], ks, cap), outs) for j in range(2)]
    mixed[...] = (gate[:, 2:3] * entry[0] + gate[:, 3:4] * entry[1]).astype(BF16)
    cotangent = up[...].astype(F32)
    sums = [jnp.sum(cotangent * e, axis=1, keepdims=True) for e in entry]
    spot = lax.broadcasted_iota(jnp.int32, (tok_dev, 128), 1)
    side = jnp.where(spot == 0, sums[0], jnp.where(spot == 1, sums[1], 0.0))
    inner[...] = jnp.transpose(side)[:2, :]


def grad_kernel(pick, early, *refs, ks):
    blocks, grad_hbm, grad, sem = refs[:-3], *refs[-3:]
    cap = blocks[0].shape[1]
    both = columns_of(pick[0] + pick[1], ks, cap)
    grad[...] = (early[...] + dot(both, jnp.concatenate([b[1] for b in blocks], axis=0))).astype(BF16)
    copy = pltpu.make_async_copy(grad, grad_hbm, sem)
    copy.start()
    copy.wait()


LAST = (7, 3)


def combine(pick, gate, upstream, blocks):
    tok_dev = pick.shape[1]
    width = blocks[0].shape[2]
    before = tuple(k for k in blocks if k not in LAST)
    first, last = [blocks[k] for k in before], [blocks[k] for k in LAST]
    vmem, anywhere = pl.BlockSpec(memory_space=pltpu.VMEM), pl.BlockSpec(memory_space=pl.ANY)
    full = jax.ShapeDtypeStruct((tok_dev, width), BF16)
    scratch = [pltpu.VMEM((tok_dev, width), BF16), pltpu.SemaphoreType.DMA]
    params = pltpu.CompilerParams(vmem_limit_bytes=VMEM_LIMIT)
    entries, early = pl.pallas_call(
        functools.partial(early_kernel, ks=before),
        out_shape=[
            jax.ShapeDtypeStruct((2, tok_dev, width), F32),
            jax.ShapeDtypeStruct((tok_dev, width), F32),
        ],
        in_specs=[vmem] * (1 + len(first)),
        out_specs=[vmem, vmem],
        compiler_params=params,
        cost_estimate=COST,
        name="early",
    )(pick, *first)
    mixed, inner = pl.pallas_call(
        functools.partial(mixed_kernel, ks=LAST),
        out_shape=[full, jax.ShapeDtypeStruct((2, tok_dev), F32)],
        in_specs=[vmem] * (4 + len(last)),
        out_specs=[vmem, vmem],
        compiler_params=params,
        cost_estimate=COST,
        name="mixed",
    )(pick, gate, upstream, entries, *last)
    grad = pl.pallas_call(
        functools.partial(grad_kernel, ks=LAST),
        out_shape=full,
        in_specs=[vmem] * (2 + len(last)),
        out_specs=anywhere,
        scratch_shapes=scratch,
        compiler_params=params,
        cost_estimate=pl.CostEstimate(flops=0, bytes_accessed=16 << 20, transcendentals=0),
        name="grad",
    )(pick, early, *last)
    return mixed, grad, inner


CHUNKS = {"A": (0, 1, 4), "B": (2, 5), "C": (3, 6), "D": (7,)}


def body_fast(tokens, upstream, gates, expert_ids, w_gate, w_up, w_down):
    count, n_tensor = lax.axis_size("expert"), lax.axis_size("tensor")
    tok_dev, width = tokens.shape
    cap = 3 * tok_dev // count
    me, t = lax.axis_index("expert"), lax.axis_index("tensor")
    info = jnp.stack([me, t]).astype(jnp.int32)
    wg, wu, wd, tokens, upstream, ids_t, gates_t = (
        pltpu.with_memory_space_constraint(a, pltpu.HBM)
        for a in (w_gate[0], w_up[0], w_down[0], tokens, upstream, expert_ids.T, gates.T)
    )
    v = {}

    def sync(*names):
        v.update(zip(names, lax.optimization_barrier(tuple(v[n] for n in names))))

    def across(k, source, result):
        with jax.named_scope(f"{result}_{k}"):
            v[f"{result}{k}"] = lax.ppermute(v[f"{source}{k}"], "expert", [(i, i ^ k) for i in range(count)])

    def swap(value, k):
        return lax.ppermute(value, "tensor", [(i, i ^ k) for i in range(n_tensor)])

    def take(*ks):
        for k in ks:
            across(k, "send", "in")

    def forward(*ks):
        for k in ks:
            with jax.named_scope(f"forward_{k}"):
                v[f"fw{k}"] = swap(v[f"in{k}"], 2)

    def weights():
        return (v["wgu"], v["wd"], v["wguo"], v["wdo"])

    def project_chunk(c):
        blocks = CHUNKS[c]
        v[f"mine{c}"], sent = project(
            [v[f"in{k}"] for k in blocks], [v[f"fw{k}"] for k in blocks], weights()
        )
        v[f"other{c}"] = swap(sent, 1)

    def partner_chunk(c):
        blocks = CHUNKS[c]
        *pay, v[f"h{c}"] = partner_part(v[f"mine{c}"], v[f"other{c}"], weights(), width, len(blocks))
        v.update({f"part{k}": p for k, p in zip(blocks, pay)})

    def own_chunk(c):
        blocks = CHUNKS[c]
        own = own_part(v[f"h{c}"], weights(), width, len(blocks))
        v.update({f"own{k}": p for k, p in zip(blocks, own)})

    def pay(*ks):
        for k in ks:
            with jax.named_scope(f"pay_{k}"):
                v[f"pay{k}"] = swap(v[f"part{k}"], 2)

    def give(*ks):
        for k in ks:
            v[f"sum{k}"] = merge(v[f"own{k}"], v[f"pay{k}"])
            if k:
                across(k, "sum", "out")
            else:
                v["out0"] = v["sum0"]

    *sends, cut_gu, cut_d = dispatch(
        info, ids_t, gates_t, tokens, upstream, wg, wu, wd, count, cap
    )
    v.update({f"send{k}": s for k, s in enumerate(sends)})
    v["in0"] = v["send0"]
    take(4, 1)
    forward(0)
    v["wguo"], v["wdo"] = swap(cut_gu, 1), swap(cut_d, 1)
    v["wgu"], v["wd"], pick, gate = cut_own(
        info, expert_ids.T, gates.T, wg, wu, wd, width, count, cap
    )
    sync("in1", "fw0", "send2", "wgu", "wd")
    take(2)
    forward(1)
    sync("in4", "send5")
    take(5)
    forward(4)
    sync("fw1", "in2", "send3", "wguo", "wdo")
    forward(2)
    take(3)
    project_chunk("A")
    sync("in5", "send6", "fw4")
    take(6)
    forward(5)
    partner_chunk("A")
    sync("fw2", "part4")
    pay(4)
    sync("in6", "send7", "part4")
    take(7)
    own_chunk("A")
    sync("pay4", "in3")
    forward(3)
    sync("fw5", "in6")
    forward(6)
    project_chunk("B")
    give(4)
    partner_chunk("B")
    own_chunk("B")
    sync("fw3", "part5")
    pay(5)
    sync("fw6", "in7")
    forward(7)
    project_chunk("C")
    partner_chunk("C")
    own_chunk("C")
    sync("fw7", "part6")
    pay(6)
    project_chunk("D")
    partner_chunk("D")
    sync("pay5", "part1", "own5", "out4")
    give(5)
    pay(1)
    sync("pay6", "part7", "own6")
    give(6)
    pay(7)
    own_chunk("D")
    sync("pay1", "part2")
    give(1)
    pay(2)
    sync("pay7", "part3", "own7")
    give(7)
    pay(3)
    sync("pay2", "part0", "out5")
    give(2)
    pay(0)
    sync("pay3", "out1")
    give(3, 0)
    mixed, grad_tokens, inner = combine(pick, gate, upstream, {k: v[f"out{k}"] for k in range(count)})
    others = [swap(inner, k) for k in range(1, n_tensor)]
    return (mixed, grad_tokens, sum(others, inner).T)


def solution(mesh):
    fast = mesh.shape["expert"] == 8 and mesh.shape["tensor"] == 4
    return jax.shard_map(
        body_fast if fast else body_general,
        mesh=mesh,
        in_specs=(
            P("expert", "tensor"),
            P("expert", "tensor"),
            P("expert", None),
            P("expert", None),
            P("expert", None, "tensor"),
            P("expert", None, "tensor"),
            P("expert", "tensor", None),
        ),
        out_specs=(P("expert", "tensor"), P("expert", "tensor"), P("expert", None)),
        check_vma=False,
    )
```
